32 devices in a mesh: src: 8 (over z, y), snk: 4 (over x, core).
Axes of the slice: x: 2, y: 2, z: 4, core: 2. Of those that a mesh axis runs over, the one named last changes fastest.
Arguments:
- tau_cols: bfloat16 [2, 8, 8, 256, 256], P(None, 'src', None, 'snk'), may hold values from -0.25 to 0.25
- elementals: bfloat16 [256, 2, 256, 256], P('src'), may hold values from -0.25 to 0.25
- need_ids: int32 [8, 8], replicated, may hold values from 0 to 255, as said below
- diagrams: int32 [8, 8, 3], P('src'), may hold values from 0 to 15, as said below
- phases: int32 [16], replicated, may hold values from 0 to 3
- block_sizes: int32 [4], replicated, may hold values from 1 to 3, 8 in all
Outputs:
- correlators: float32 [8, 4, 3, 2, 8], P('src', 'snk')
The draws below stay inside these ranges and needn't reach their ends.
Inputs may be any that keep to these rules, and one draw needn't show every extreme that they name: `block_sizes`: the sizes sum to 8, and one of them is exactly 3. `need_ids`: the 8 ids of a row are distinct. `diagrams`: entry 0 of a diagram is below 4, entry 1 below 4, entry 2 below 16; each of a row's 4 sink-side and 4 source-side entries is named by some diagram of the row.
All inputs are finite; a program needn't handle non-finite values.
Results may differ from the reference program's by a relative error of at most 0.004.
Values may be sent and summed in bfloat16 or wider, within the bound.
A program may use at most 64 MiB of HBM per device.

```python
import math
import jax
import jax.numpy as jnp
import numpy as np
from jax import lax

NV = 256
NE = 256
NSN = 4
NSR = 4
NI = 8
NDIAG = 8
NGAM = 16
MAXB = 3
TSNK = 8
TSRC = 8
N_SRC = 8
N_SNK = 4


def draw_need_ids(key, part):
    row_keys = jax.random.split(key, N_SRC)

    def one_row(row_key):
        return jax.random.permutation(row_key, NE)[:NI].astype(jnp.int32)
    table_rows = jax.vmap(one_row)(row_keys)
    leading = jnp.array([NE - 1, 0], dtype=jnp.int32)
    middle = (jax.random.permutation(jax.random.fold_in(key, 7), NE - 2)[:NI - 2] + 1).astype(jnp.int32)
    return table_rows.at[0].set(jnp.concatenate([leading, middle]))


def draw_diagrams(key, part):
    first_key, second_key, third_key, fourth_key = jax.random.split(jax.random.fold_in(key, 11), 4)
    places = jnp.arange(NDIAG, dtype=jnp.int32)[None, :]
    sink_free = jax.random.randint(first_key, (N_SRC, NDIAG), 0, NSN, dtype=jnp.int32)
    source_free = jax.random.randint(second_key, (N_SRC, NDIAG), 0, NSR, dtype=jnp.int32)
    rotation = jax.random.randint(third_key, (N_SRC, 1), 0, NSR, dtype=jnp.int32)
    sink_column = jnp.where(places < NSN, places % NSN, sink_free)
    source_column = jnp.where(places < NSR, (places + rotation) % NSR, source_free)
    gamma_column = jax.random.randint(fourth_key, (N_SRC, NDIAG), 0, NGAM, dtype=jnp.int32)
    gamma_column = gamma_column.at[0, 0].set(NGAM - 1)
    return jnp.stack([sink_column, source_column, gamma_column], axis=2).astype(jnp.int32)


def place_ends(values, stream_key, low, high):
    longest = values.shape.index(max(values.shape))
    spots = []
    for shift in (0, 1):
        where = [jax.random.randint(jax.random.fold_in(stream_key, axis), (), 0, length) for axis, length in enumerate(values.shape)]
        where[longest] = (where[longest] + shift) % values.shape[longest]
        spots.append(tuple(where))
    return values.at[spots[0]].set(low).at[spots[1]].set(high)


def level_of(own_key, extent, pieces, low, top_value):
    def one(axis_at, shards_of):
        heights = jax.random.uniform(jax.random.fold_in(jax.random.fold_in(own_key, 6), axis_at), (shards_of,), jnp.float32, low / len(pieces), top_value / len(pieces))
        return jnp.repeat(jnp.exp(heights), extent[axis_at] // shards_of).reshape((-1,) + (1,) * (len(extent) - axis_at - 1))

    level = one(*pieces[0])
    for cut in pieces[1:]:
        level = level * one(*cut)
    return level


def split_up(number_of, total, most, skew):
    weights = [(1 << 20) // math.isqrt(rank ** skew) + 1 for rank in range(2, number_of + 1)]
    spare, holding = total - most - (number_of - 1), [1] * (number_of - 1)
    while spare > 0:
        movable = [i for i in range(number_of - 1) if holding[i] < most]
        mass, left = sum([weights[i] for i in movable]), spare
        for i in movable:
            addition = min(most - holding[i], max(1, left * weights[i] // mass), spare)
            holding[i] = holding[i] + addition
            spare = spare - addition
    return np.array([most] + holding)


def ragged_sizes(key, amount, total, bound, lean):
    if amount == 2:
        one = jax.random.randint(key, (), max(1, total - bound), min(bound, total - 1) + 1)
        return jnp.stack([one, total - one])
    sizes = jnp.asarray(split_up(amount, total, bound, lean), jnp.int32)
    twos = (amount - 1) // 2
    source_of, taker = sizes[1:1 + 2 * twos:2], sizes[2:2 + 2 * twos:2]
    margin = jnp.minimum(source_of - 1, bound - taker)
    shifted = jax.random.randint(jax.random.fold_in(key, 1), (twos,), 0, 1 << 20) % (margin + 1)
    sizes = sizes.at[1:1 + 2 * twos:2].set(source_of - shifted).at[2:2 + 2 * twos:2].set(taker + shifted)
    return sizes[jax.random.permutation(jax.random.fold_in(key, 2), amount)]


def bell_draw(own_key, extent, deviation, most, shards=(), kind=jnp.bfloat16):
    loudness = level_of(own_key, extent, shards, -0.22, 0.18) if shards else 1.0
    drawn = jax.random.normal(own_key, extent, jnp.float32) * deviation * loudness
    return jnp.minimum(jnp.maximum(drawn, -most), most).astype(kind)


def setup_inputs(seed: int = 0) -> dict:
    splits = jax.random.split(jax.random.key(seed), 7)
    return {
        "tau_cols": bell_draw(splits[0], (2, TSRC, TSNK, NV, NV), (2 * NV) ** -0.5, 0.25, ((1, 8), (3, 4))),
        "elementals": bell_draw(splits[1], (NV, 2, NE, NV), (2 * NV) ** -0.5, 0.25, ((0, 8),)),
        "need_ids": draw_need_ids(jax.random.fold_in(splits[6], 71), 0),
        "diagrams": draw_diagrams(jax.random.fold_in(splits[6], 71), 0),
        "phases": place_ends(jax.random.randint(splits[4], (NGAM,), 0, 4), jax.random.fold_in(splits[4], 1), 0, 3).astype(jnp.int32),
        "block_sizes": ragged_sizes(splits[5], N_SNK, TSNK, MAXB, 2).astype(jnp.int32),
    }


def slot_values(elemental_items, tau_slot, diagram_rows, phases):
    real_part = tau_slot[0]
    imag_part = tau_slot[1]
    left_stack = jnp.stack([jnp.stack([real_part, imag_part]), jnp.stack([-imag_part, real_part])]).astype(jnp.float32)
    right_stack = jnp.stack([jnp.stack([real_part, -imag_part]), jnp.stack([imag_part, real_part])]).astype(jnp.float32)
    items_wide = elemental_items.astype(jnp.float32)
    left_node = lax.dot_general(items_wide[:, :, :NSN], left_stack, (((1, 3), (0, 3)), ((), ())), precision=lax.Precision.HIGHEST)
    left_node = lax.optimization_barrier(left_node.astype(jnp.bfloat16)).astype(jnp.float32)
    right_node = lax.dot_general(items_wide[:, :, NSN:], right_stack, (((1, 3), (0, 2)), ((), ())), precision=lax.Precision.HIGHEST)
    right_node = lax.optimization_barrier(right_node.astype(jnp.bfloat16)).astype(jnp.float32)
    pair_sums = lax.dot_general(left_node, right_node, (((0, 3), (3, 0)), ((), ())), precision=lax.Precision.HIGHEST)
    pair_real = pair_sums[:, 0, :, 0] - pair_sums[:, 1, :, 1]
    pair_imag = pair_sums[:, 0, :, 1] + pair_sums[:, 1, :, 0]
    chosen_real = pair_real[diagram_rows[:, 0], diagram_rows[:, 1]]
    chosen_imag = pair_imag[diagram_rows[:, 0], diagram_rows[:, 1]]
    quarter = phases[diagram_rows[:, 2]]
    cosine = (quarter == 0).astype(jnp.float32) - (quarter == 2).astype(jnp.float32)
    sine_part = (quarter == 1).astype(jnp.float32) - (quarter == 3).astype(jnp.float32)
    return jnp.stack([cosine * chosen_real - sine_part * chosen_imag, sine_part * chosen_real + cosine * chosen_imag])


def reference(tau_cols, elementals, need_ids, diagrams, phases, block_sizes):
    def per_source(source):
        elemental_items = jnp.take(elementals, need_ids[source], axis=2)
        diagram_rows = diagrams[source]
        source_tau = lax.dynamic_index_in_dim(tau_cols, source, axis=1, keepdims=False)

        def per_time(sink_time):
            tau_slot = lax.dynamic_index_in_dim(source_tau, sink_time, axis=1, keepdims=False)
            return slot_values(elemental_items, tau_slot, diagram_rows, phases)

        return lax.map(per_time, jnp.arange(TSNK, dtype=jnp.int32))

    values = lax.map(per_source, jnp.arange(N_SRC, dtype=jnp.int32))
    starts = (jnp.cumsum(block_sizes) - block_sizes).astype(jnp.int32)
    offsets = jnp.arange(MAXB, dtype=jnp.int32)
    filled = offsets[None, :] < block_sizes[:, None]
    sink_times = jnp.where(filled, starts[:, None] + offsets[None, :], 0).astype(jnp.int32)
    picked = jnp.take(values, sink_times, axis=1)
    return picked * filled[None, :, :, None, None].astype(values.dtype)
```

```python
import functools

import jax
import jax.numpy as jnp
from jax import lax
from jax.experimental import pallas as pl
from jax.experimental.pallas import tpu as pltpu
from jax.sharding import PartitionSpec as P

NSN = 4
MAXB = 3


def slot_values(gathered, tau_slot, diagram_rows, phases):
    real_part = tau_slot[0]
    imag_part = tau_slot[1]
    left_stack = jnp.stack([jnp.stack([real_part, imag_part]), jnp.stack([-imag_part, real_part])])
    right_stack = jnp.stack([jnp.stack([real_part, -imag_part]), jnp.stack([imag_part, real_part])])
    left_node = lax.dot_general(
        gathered[:, :, :NSN],
        left_stack,
        (((1, 3), (0, 3)), ((), ())),
        preferred_element_type=jnp.float32,
    ).astype(jnp.bfloat16)
    right_node = lax.dot_general(
        gathered[:, :, NSN:],
        right_stack,
        (((1, 3), (0, 2)), ((), ())),
        preferred_element_type=jnp.float32,
    ).astype(jnp.bfloat16)
    pair_sums = lax.dot_general(
        left_node, right_node, (((0, 3), (3, 0)), ((), ())), preferred_element_type=jnp.float32
    )
    pair_real = pair_sums[:, 0, :, 0] - pair_sums[:, 1, :, 1]
    pair_imag = pair_sums[:, 0, :, 1] + pair_sums[:, 1, :, 0]
    sink_pick = (
        diagram_rows[:, 0:1] == jnp.arange(pair_real.shape[0], dtype=jnp.int32)[None, :]
    ).astype(jnp.float32)
    source_pick = (
        diagram_rows[:, 1:2] == jnp.arange(pair_real.shape[1], dtype=jnp.int32)[None, :]
    ).astype(jnp.float32)
    chosen_real = jnp.sum(
        sink_pick[:, :, None] * pair_real[None] * source_pick[:, None, :], axis=(1, 2)
    )
    chosen_imag = jnp.sum(
        sink_pick[:, :, None] * pair_imag[None] * source_pick[:, None, :], axis=(1, 2)
    )
    gamma_pick = diagram_rows[:, 2:3] == jnp.arange(phases.shape[0], dtype=jnp.int32)[None, :]
    quarter = jnp.sum(jnp.where(gamma_pick, phases[None, :], 0), axis=1)
    cosine = (quarter == 0).astype(jnp.float32) - (quarter == 2).astype(jnp.float32)
    sine_part = (quarter == 1).astype(jnp.float32) - (quarter == 3).astype(jnp.float32)
    return jnp.stack(
        [
            cosine * chosen_real - sine_part * chosen_imag,
            sine_part * chosen_real + cosine * chosen_imag,
        ]
    )


def plain_local(tau_cols, elementals, need_ids, diagrams, phases, block_sizes):
    groups = lax.axis_size("snk")
    column = lax.axis_index("snk")
    full_width = tau_cols.shape[4]
    col_count = tau_cols.shape[3]
    sink_count = tau_cols.shape[2]
    diagram_rows = diagrams[0]
    block_at = jnp.arange(block_sizes.shape[0], dtype=jnp.int32)
    starts = jnp.sum(
        jnp.where(block_at[None, :] < block_at[:, None], block_sizes[None, :], 0), axis=1
    )
    offsets = jnp.arange(MAXB, dtype=jnp.int32)
    picked = jnp.take(elementals, need_ids, axis=2)
    arrived = lax.all_to_all(picked, "src", split_axis=2, concat_axis=0, tiled=True)
    gathered = arrived.reshape(full_width, 2, need_ids.shape[1], full_width)
    local_tau = tau_cols[:, 0]
    per_group = sink_count // groups
    half_turn = groups // 2
    packed = local_tau.reshape(2, groups, per_group, col_count, full_width)
    packed = jnp.roll(packed, -half_turn, axis=1)
    arrived_tau = lax.all_to_all(packed, "snk", split_axis=1, concat_axis=3, tiled=True)
    blocks = arrived_tau.reshape(2, per_group, full_width, full_width)
    results = jnp.stack(
        [
            slot_values(gathered, blocks[:, place], diagram_rows, phases)
            for place in range(per_group)
        ]
    )
    all_values = lax.all_gather(results, "snk", axis=0, tiled=True)
    all_values = jnp.roll(all_values, half_turn * per_group, axis=0)
    own_start = lax.dynamic_index_in_dim(starts, column, keepdims=False)
    own_size = lax.dynamic_index_in_dim(block_sizes, column, keepdims=False)
    own_filled = offsets < own_size
    own_times = jnp.where(own_filled, own_start + offsets, 0)
    wanted = own_filled[:, None] & (
        own_times[:, None] == jnp.arange(all_values.shape[0], dtype=jnp.int32)[None, :]
    )
    correlators = jnp.sum(jnp.where(wanted[:, :, None, None], all_values[None], 0.0), axis=1)
    return correlators.reshape(1, 1, MAXB, 2, diagram_rows.shape[0])


MESH = pl.DeviceIdType.MESH
HALF = 4
WINDOW = 4
NT = (((1,), (1,)), ((), ()))
NN = (((1,), (0,)), ((), ()))


def flipped(value, mask):
    for bit in (1, 2, 4):
        if mask & bit:
            value = value + bit * (1 - 2 * ((value // bit) % 2))
    return value


def kernel(
    ids_hbm, diag_hbm, phase_hbm, size_hbm, tau_ref, el_ref, out_ref,
    ids_ref, diag_ref, phase_ref, size_ref,
    table, pick, sendbuf, sendother, sink_rows, source_rows, xbuf,
    spun, turned, right_pos, right_neg, xmat, staged, sums, vbuf, total,
    small_sem, tab_sem, own_sem, tau_own, tau_send, tau_recv, tau_pass_send, tau_pass_recv,
    direct_send, direct_recv, far_send, far_recv, on_send, on_recv, near_send, near_recv,
    val_send, val_recv,
):
    s = lax.axis_index("src")
    c = lax.axis_index("snk")
    x, h = c // 2, c % 2
    n_src, n_ids = ids_ref.shape
    rows, ne, nv = table.shape[1:]
    times = xbuf.shape[1]
    f32, bf16 = jnp.float32, jnp.bfloat16
    base = (s // HALF) * HALF
    near, across = flipped(c, 1), flipped(c, 2)
    n_sink, n_source = sink_rows.shape[2], source_rows.shape[3]
    ids_of = (pl.ds(n_sink, n_source), pl.ds(0, n_sink))

    smalls = []
    for n, (there, here) in enumerate(
        ((ids_hbm, ids_ref), (diag_hbm, diag_ref), (phase_hbm, phase_ref), (size_hbm, size_ref))
    ):
        smalls.append(pltpu.make_async_copy(there, here, small_sem.at[n]))
        smalls[-1].start()
    parts = (x, 1 - x)
    table_in = []
    for n, part in enumerate(parts):
        table_in.append(
            pltpu.make_async_copy(el_ref.at[pl.ds(h * rows, rows), part], table.at[n], tab_sem.at[n])
        )
        table_in[-1].start()

    barrier = pltpu.get_barrier_semaphore()
    for m in range(1, n_src):
        pl.semaphore_signal(barrier, 1, device_id=(flipped(s, m), c), device_id_type=MESH)
    for m in range(1, 4):
        pl.semaphore_signal(barrier, 1, device_id=(s, flipped(c, m)), device_id_type=MESH)

    def tau_part(owner):
        return tau_ref.at[:, 0, pl.ds(owner * times, times)]

    tau_in = pltpu.make_async_copy(tau_part(x), xbuf.at[:, :, c], tau_own)
    tau_in.start()

    sub = lax.broadcasted_iota(jnp.int32, (n_ids, ne), 0)
    lane = lax.broadcasted_iota(jnp.int32, (n_ids, ne), 1)
    smalls[0].wait()

    def one_hot(owners):
        hots = []
        for i in owners:
            wanted = jnp.zeros((n_ids, ne), jnp.int32)
            for k in range(n_ids):
                wanted = jnp.where(sub == k, ids_ref[i, k], wanted)
            hots.append((wanted == lane).astype(f32))
        return jnp.concatenate(hots, axis=0).astype(bf16)

    def pick_rows(n, hot, target):
        count = target.shape[0] * n_ids
        for r in range(rows):
            got = lax.dot_general(hot, table[n, r], NN, preferred_element_type=f32)
            for side in range(nv // 128):
                pick[side, pl.ds(r, count, stride=rows), :] = got[:, side * 128:(side + 1) * 128]
        for i in range(target.shape[0]):
            for side in range(nv // 128):
                target[i, :, :, side * 128:(side + 1) * 128] = (
                    pick[side, pl.ds(i * n_ids * rows, n_ids * rows), :]
                    .astype(bf16)
                    .reshape(n_ids, rows, 128)
                )

    def remote(src, dst, send, recv, device):
        return pltpu.make_async_remote_copy(
            src_ref=src, dst_ref=dst, send_sem=send, recv_sem=recv,
            device_id=device, device_id_type=MESH,
        )

    started = []

    def go(copy):
        copy.start()
        started.append(copy)
        return copy

    def place(kind, part, source):
        return source_rows.at[part, h, source] if kind == 0 else sink_rows.at[part, source]

    hot = one_hot(range(n_src))
    table_in[0].wait()
    pick_rows(0, hot, sendbuf)

    depth, lane_y = s // 2, s % 2
    inner = ((depth + 1) // 2) % 2
    other_half = 1 - depth // 2
    inner_at, outer_at = 1 + other_half, 3 * other_half

    far = []
    for kind in (0, 1):
        for y_flip in (0, 1):
            for n, there in ((1, outer_at), (0, inner_at)):
                peer = there * 2 + flipped(lane_y, y_flip)
                far.append(remote(
                    sendbuf.at[peer, ids_of[kind]], place(kind, x, s),
                    far_send.at[kind, 2 * n + y_flip], far_recv.at[kind, 2 * (1 - inner) + y_flip],
                    (peer, c),
                ))

    direct = {}

    def send_direct(n, chunk_of):
        for kind in (0, 1):
            for m in (2, 3, 1):
                direct[n, kind, m] = remote(
                    chunk_of(flipped(s, m)).at[ids_of[kind]], place(kind, parts[n], s),
                    direct_send.at[n, kind, m], direct_recv.at[n, kind, m], (flipped(s, m), c),
                )
                go(direct[n, kind, m])

    own = {}

    def keep_own(n, chunk):
        for kind in (0, 1):
            own[n, kind] = pltpu.make_async_copy(
                chunk.at[ids_of[kind]], place(kind, parts[n], s), own_sem.at[n, kind]
            )
            own[n, kind].start()

    pl.semaphore_wait(barrier, n_src - 1 + 3)

    tau_out = {}

    def send_tau(m, owner):
        tau_out[m] = go(remote(
            tau_part(owner), xbuf.at[:, :, c], tau_send.at[m], tau_recv.at[m], (s, flipped(c, m)),
        ))

    for j in range(WINDOW):
        go(far[j])
    send_tau(2, 1 - x)
    send_direct(0, lambda i: sendbuf.at[i])
    send_tau(1, x)
    keep_own(0, sendbuf.at[s])
    table_in[1].wait()
    pick_rows(1, one_hot([base + i for i in range(HALF)]), sendother)
    send_direct(1, lambda i: sendother.at[i - base])
    keep_own(1, sendother.at[s - base])

    def far_source(q):
        return (inner_at, outer_at)[q // 2] * 2 + flipped(lane_y, q % 2)

    near_in = []

    def to_near(ref, at):
        near_in.append(go(remote(ref, ref, near_send.at[at], near_recv.at[at], (s, near))))

    def pass_half(n):
        own[n, 0].wait()
        for m in (1, 2, 3):
            direct[n, 0, m].wait_recv()
        to_near(source_rows.at[parts[n], h, pl.ds(base, HALF)], n)

    relayed = {}
    sent = []

    def relay(kind, q):
        if len(sent) + WINDOW < len(far):
            far[len(sent)].wait_send()
            go(far[len(sent) + WINDOW])
        sent.append(q)
        chunk = place(kind, x, far_source(q))
        remote(chunk, chunk, on_send.at[kind, q], far_recv.at[kind, q], (s, across)).wait_recv()
        relayed[kind, q] = go(remote(
            chunk, chunk, on_send.at[kind, q], on_recv.at[kind, q], (s, across)
        ))
        if kind == 0:
            to_near(chunk, 2 + q)

    def pass_on(q):
        relayed[0, q].wait_recv()
        to_near(place(0, 1 - x, far_source(q)), 6 + q)

    def pass_tau():
        tau_out[2].wait_recv()
        theirs = xbuf.at[:, :, across]
        tau_out[3] = go(remote(theirs, theirs, tau_pass_send, tau_pass_recv, (s, near)))

    def turn_tau():
        tau_in.wait()
        tau_out[1].wait_recv()
        tau_out[3].wait_recv()
        blocks = nv // rows

        def one(t, carry):
            for part in (0, 1):
                spun[part] = jnp.transpose(xbuf[part, t].reshape(nv, nv)).reshape(blocks, rows, nv)
            for i in range(n_src):
                down = slice(i * rows, (i + 1) * rows)
                re, im = spun[0, 2 * i + h], spun[1, 2 * i + h]
                turned[0, t, 0, down] = re
                turned[0, t, 1, down] = -im
                turned[1, t, 0, down] = im
                turned[1, t, 1, down] = re
            return carry

        lax.fori_loop(0, times, one, 0)

    def mm(a, b, dims):
        return lax.dot_general(a, b, dims, preferred_element_type=f32)

    def stacked(part, k):
        return jnp.concatenate(
            [source_rows[part, side, i, k] for i in range(n_src) for side in range(2)], axis=0
        )

    mid = nv // 2

    def rights(k, carry):
        e_re, e_im = stacked(0, k), stacked(1, k)
        for t in range(times):
            got = (
                mm(turned[0, t].reshape(nv, nv), e_re, NT) + mm(turned[1, t].reshape(nv, nv), e_im, NT)
            ).astype(bf16)
            right_pos[t, k, 0] = got[:mid]
            right_pos[t, k, 1] = got[mid:]
            right_neg[t, k, 0] = -got[mid:]
            right_neg[t, k, 1] = got[:mid]
        return carry

    def wholes(t, carry):
        x_re, x_im = xbuf[0, t].reshape(nv, nv), xbuf[1, t].reshape(nv, nv)
        for k in range(n_source):
            got = mm(right_pos[t, k].reshape(nv, nv), x_re, NN) + mm(
                right_neg[t, k].reshape(nv, nv), x_im, NN
            )
            xmat[t, k, 0] = got[:mid]
            xmat[t, k, 1] = got[mid:]
        return carry

    n_diag = diag_ref.shape[2]
    zero = jnp.zeros((8, 128), f32)

    def products(sources, first):
        for n, i in enumerate(sources):
            for part in (0, 1):
                for k in range(n_sink):
                    staged[n, part, k] = sink_rows[part, i, k].astype(f32)

        def one(d, carry):
            k1, k2 = diag_ref[0, 0, d], diag_ref[1, 0, d]
            acc = [zero if first else sums[d, n] for n in range(2 * times)]
            for n, i in enumerate(sources):
                e_re, e_im = staged[n, 0, k1], staged[n, 1, k1]
                down = pl.ds(pl.multiple_of(i * rows, rows), rows)
                for t in range(times):
                    x_re, x_im = xmat[t, k2, 0, down, :], xmat[t, k2, 1, down, :]
                    re = e_re * x_re - e_im * x_im
                    im = e_re * x_im + e_im * x_re
                    for m, value in ((2 * t, re), (2 * t + 1, im)):
                        for r in range(rows // 8):
                            for l in range(nv // 128):
                                acc[m] = acc[m] + value[r * 8:(r + 1) * 8, l * 128:(l + 1) * 128]
            for n in range(2 * times):
                sums[d, n] = acc[n]
            return carry

        lax.fori_loop(0, n_diag, one, 0)

    relay(0, 0)
    relay(0, 2)
    pass_half(0)
    relay(0, 1)
    pass_on(0)
    relay(0, 3)
    pass_on(2)
    pass_half(1)
    pass_tau()
    relay(1, 0)
    pass_on(1)
    relay(1, 2)
    pass_on(3)
    turn_tau()
    relay(1, 1)
    for copy in near_in:
        copy.wait_recv()
    lax.fori_loop(0, n_source, rights, 0)
    relay(1, 3)
    lax.fori_loop(0, times, wholes, 0)

    for copy in smalls[1:]:
        copy.wait()
    for n in (0, 1):
        own[n, 1].wait()
        for m in (1, 2, 3):
            direct[n, 1, m].wait_recv()
    products([base + i for i in range(HALF)], True)
    for q in (0, 2, 1, 3):
        relayed[1, q].wait_recv()
        products([far_source(q)], False)

    values = []
    for t in range(times):
        real, imag = [], []
        for d in range(n_diag):
            turn = phase_ref[diag_ref[2, 0, d]]
            cosine = (turn == 0).astype(f32) - (turn == 2).astype(f32)
            sine = (turn == 1).astype(f32) - (turn == 3).astype(f32)
            re = jnp.sum(sums[d, 2 * t], axis=0, keepdims=True)
            im = jnp.sum(sums[d, 2 * t + 1], axis=0, keepdims=True)
            real.append(cosine * re - sine * im)
            imag.append(sine * re + cosine * im)
        values += real + imag
    flat = jnp.sum(jnp.transpose(jnp.concatenate(values, axis=0)), axis=0, keepdims=True)
    width = 2 * n_diag
    sub8 = lax.broadcasted_iota(jnp.int32, (8, width), 0)
    tile = jnp.zeros((8, width), f32)
    for t in range(times):
        tile = jnp.where(sub8 == x * times + t, flat[:, t * width:(t + 1) * width], tile)
    vbuf[c, :, :width] = tile

    val_out = []
    for m in (2, 3, 1):
        val_out.append(go(remote(
            vbuf.at[c], vbuf.at[c], val_send.at[m], val_recv.at[m], (s, flipped(c, m)),
        )))
    for copy in val_out:
        copy.wait_recv()

    whole = vbuf[0, :, :width]
    for n in range(1, vbuf.shape[0]):
        whole = whole + vbuf[n, :, :width]
    total[:, :width] = whole
    first, size = 0, 0
    for j in range(size_ref.shape[0]):
        first = first + jnp.where(j < c, size_ref[j], 0)
        size = size + jnp.where(j == c, size_ref[j], 0)
    for at_place in range(MAXB):
        at = jnp.minimum(first + at_place, total.shape[0] - 1)
        keep = (at_place < size).astype(f32)
        row = total[pl.ds(at, 1), :width] * keep
        out_ref[at_place, 0:1, :] = row[:, :n_diag]
        out_ref[at_place, 1:2, :] = row[:, n_diag:]

    waited = len(far) - WINDOW
    for copy in started:
        if not any(copy is one for one in far[:waited]):
            copy.wait_send()


def fused_local(tau_cols, elementals, need_ids, diagrams, phases, block_sizes):
    n_snk = lax.axis_size("snk")
    n_src, n_ids = need_ids.shape
    own_rows, _, ne, nv = elementals.shape
    sinks, cols = tau_cols.shape[2], tau_cols.shape[3]
    times = sinks // 2
    rows = own_rows // 2
    n_diag = diagrams.shape[1]
    n_right = n_ids - NSN
    bf16, f32 = jnp.bfloat16, jnp.float32
    sem = pltpu.SemaphoreType.DMA
    i32 = jnp.int32
    held = pl.BlockSpec(memory_space=pltpu.HBM)
    values = pl.pallas_call(
        kernel,
        out_shape=jax.ShapeDtypeStruct((MAXB, 2, n_diag), f32),
        in_specs=[held] * 6,
        out_specs=pl.BlockSpec(memory_space=pltpu.VMEM),
        scratch_shapes=[
            pltpu.SMEM((n_src, n_ids), i32),
            pltpu.SMEM((3, 1, n_diag), i32),
            pltpu.SMEM(phases.shape, i32),
            pltpu.SMEM(block_sizes.shape, i32),
            pltpu.VMEM((2, rows, ne, nv), bf16),
            pltpu.VMEM((nv // 128, n_src * n_ids * rows, 128), f32),
            pltpu.VMEM((n_src, n_ids, rows, nv), bf16),
            pltpu.VMEM((HALF, n_ids, rows, nv), bf16),
            pltpu.VMEM((2, n_src, NSN, rows, nv), bf16),
            pltpu.VMEM((2, 2, n_src, n_right, rows, nv), bf16),
            pltpu.VMEM((2, times, n_snk, cols, nv), bf16),
            pltpu.VMEM((2, nv // rows, rows, nv), bf16),
            pltpu.VMEM((2, times, 2, nv // 2, nv), bf16),
            pltpu.VMEM((times, n_right, 2, nv // 2, nv), bf16),
            pltpu.VMEM((times, n_right, 2, nv // 2, nv), bf16),
            pltpu.VMEM((times, n_right, 2, nv // 2, nv), f32),
            pltpu.VMEM((HALF, 2, NSN, rows, nv), f32),
            pltpu.VMEM((n_diag, 2 * times, 8, 128), f32),
            pltpu.VMEM((n_snk, 8, 128), f32),
            pltpu.VMEM((8, 128), f32),
            sem((4,)), sem((2,)), sem((2, 2)), sem, sem((4,)), sem((4,)), sem, sem,
            sem((2, 2, 4)), sem((2, 2, 4)), sem((2, 4)), sem((2, 4)), sem((2, 4)), sem((2, 4)),
            sem((10,)), sem((10,)), sem((4,)), sem((4,)),
        ],
        compiler_params=pltpu.CompilerParams(
            collective_id=0, has_side_effects=True, vmem_limit_bytes=67043328
        ),
    )(need_ids, jnp.transpose(diagrams, (2, 0, 1)), phases, block_sizes, tau_cols, elementals)
    return values.reshape(1, 1, MAXB, 2, n_diag)


def local(tau_cols, elementals, *rest):
    fits = (
        lax.axis_size("snk") == 4
        and lax.axis_size("src") == 8
        and elementals.shape[0] == 32
        and tau_cols.shape[2] == 8
        and tau_cols.shape[3] == 64
        and tau_cols.shape[4] == 256
    )
    return (fused_local if fits else plain_local)(tau_cols, elementals, *rest)


def solution(mesh):
    placed = (
        P(None, "src", None, "snk", None),
        P("src", None, None, None),
        P(),
        P("src", None, None),
        P(),
        P(),
    )
    return jax.shard_map(
        local,
        mesh=mesh,
        in_specs=placed,
        out_specs=P("src", "snk", None, None, None),
        check_vma=False,
    )
```

```python
import functools

import jax
import jax.numpy as jnp
from jax import lax
from jax.experimental import pallas as pl
from jax.experimental.pallas import tpu as pltpu
from jax.sharding import PartitionSpec as P

NSN = 4
MAXB = 3


def slot_values(gathered, tau_slot, diagram_rows, phases):
    real_part = tau_slot[0]
    imag_part = tau_slot[1]
    left_stack = jnp.stack([jnp.stack([real_part, imag_part]), jnp.stack([-imag_part, real_part])])
    right_stack = jnp.stack([jnp.stack([real_part, -imag_part]), jnp.stack([imag_part, real_part])])
    left_node = lax.dot_general(
        gathered[:, :, :NSN],
        left_stack,
        (((1, 3), (0, 3)), ((), ())),
        preferred_element_type=jnp.float32,
    ).astype(jnp.bfloat16)
    right_node = lax.dot_general(
        gathered[:, :, NSN:],
        right_stack,
        (((1, 3), (0, 2)), ((), ())),
        preferred_element_type=jnp.float32,
    ).astype(jnp.bfloat16)
    pair_sums = lax.dot_general(
        left_node, right_node, (((0, 3), (3, 0)), ((), ())), preferred_element_type=jnp.float32
    )
    pair_real = pair_sums[:, 0, :, 0] - pair_sums[:, 1, :, 1]
    pair_imag = pair_sums[:, 0, :, 1] + pair_sums[:, 1, :, 0]
    sink_pick = (
        diagram_rows[:, 0:1] == jnp.arange(pair_real.shape[0], dtype=jnp.int32)[None, :]
    ).astype(jnp.float32)
    source_pick = (
        diagram_rows[:, 1:2] == jnp.arange(pair_real.shape[1], dtype=jnp.int32)[None, :]
    ).astype(jnp.float32)
    chosen_real = jnp.sum(
        sink_pick[:, :, None] * pair_real[None] * source_pick[:, None, :], axis=(1, 2)
    )
    chosen_imag = jnp.sum(
        sink_pick[:, :, None] * pair_imag[None] * source_pick[:, None, :], axis=(1, 2)
    )
    gamma_pick = diagram_rows[:, 2:3] == jnp.arange(phases.shape[0], dtype=jnp.int32)[None, :]
    quarter = jnp.sum(jnp.where(gamma_pick, phases[None, :], 0), axis=1)
    cosine = (quarter == 0).astype(jnp.float32) - (quarter == 2).astype(jnp.float32)
    sine_part = (quarter == 1).astype(jnp.float32) - (quarter == 3).astype(jnp.float32)
    return jnp.stack(
        [
            cosine * chosen_real - sine_part * chosen_imag,
            sine_part * chosen_real + cosine * chosen_imag,
        ]
    )


def plain_local(tau_cols, elementals, need_ids, diagrams, phases, block_sizes):
    groups = lax.axis_size("snk")
    column = lax.axis_index("snk")
    full_width = tau_cols.shape[4]
    col_count = tau_cols.shape[3]
    sink_count = tau_cols.shape[2]
    diagram_rows = diagrams[0]
    block_at = jnp.arange(block_sizes.shape[0], dtype=jnp.int32)
    starts = jnp.sum(
        jnp.where(block_at[None, :] < block_at[:, None], block_sizes[None, :], 0), axis=1
    )
    offsets = jnp.arange(MAXB, dtype=jnp.int32)
    picked = jnp.take(elementals, need_ids, axis=2)
    arrived = lax.all_to_all(picked, "src", split_axis=2, concat_axis=0, tiled=True)
    gathered = arrived.reshape(full_width, 2, need_ids.shape[1], full_width)
    local_tau = tau_cols[:, 0]
    per_group = sink_count // groups
    half_turn = groups // 2
    packed = local_tau.reshape(2, groups, per_group, col_count, full_width)
    packed = jnp.roll(packed, -half_turn, axis=1)
    arrived_tau = lax.all_to_all(packed, "snk", split_axis=1, concat_axis=3, tiled=True)
    blocks = arrived_tau.reshape(2, per_group, full_width, full_width)
    results = jnp.stack(
        [
            slot_values(gathered, blocks[:, place], diagram_rows, phases)
            for place in range(per_group)
        ]
    )
    all_values = lax.all_gather(results, "snk", axis=0, tiled=True)
    all_values = jnp.roll(all_values, half_turn * per_group, axis=0)
    own_start = lax.dynamic_index_in_dim(starts, column, keepdims=False)
    own_size = lax.dynamic_index_in_dim(block_sizes, column, keepdims=False)
    own_filled = offsets < own_size
    own_times = jnp.where(own_filled, own_start + offsets, 0)
    wanted = own_filled[:, None] & (
        own_times[:, None] == jnp.arange(all_values.shape[0], dtype=jnp.int32)[None, :]
    )
    correlators = jnp.sum(jnp.where(wanted[:, :, None, None], all_values[None], 0.0), axis=1)
    return correlators.reshape(1, 1, MAXB, 2, diagram_rows.shape[0])


MESH = pl.DeviceIdType.MESH
HALF = 4
NT = (((1,), (1,)), ((), ()))
NN = (((1,), (0,)), ((), ()))


def flipped(value, mask):
    for bit in (1, 2, 4):
        if mask & bit:
            value = value + bit * (1 - 2 * ((value // bit) % 2))
    return value


def kernel(
    ids_hbm, diag_hbm, phase_hbm, size_hbm, tau_ref, el_ref, out_ref,
    ids_ref, diag_ref, phase_ref, size_ref,
    table, pick, sendbuf, sendother, sink_rows, source_rows, xbuf,
    spun, turned, right_pos, right_neg, xmat, staged, sums, vbuf, total,
    small_sem, tab_sem, own_sem, tau_own, tau_send, tau_recv, tau_pass_send, tau_pass_recv,
    direct_send, direct_recv, far_send, far_recv, on_send, on_recv, near_send, near_recv,
    val_send, val_recv,
):
    s = lax.axis_index("src")
    c = lax.axis_index("snk")
    x, h = c // 2, c % 2
    n_src, n_ids = ids_ref.shape
    rows, ne, nv = table.shape[1:]
    times = xbuf.shape[1]
    f32, bf16 = jnp.float32, jnp.bfloat16
    base = (s // HALF) * HALF
    near, across = flipped(c, 1), flipped(c, 2)
    n_sink, n_source = sink_rows.shape[2], source_rows.shape[3]
    ids_of = (pl.ds(n_sink, n_source), pl.ds(0, n_sink))

    smalls = []
    for n, (there, here) in enumerate(
        ((ids_hbm, ids_ref), (diag_hbm, diag_ref), (phase_hbm, phase_ref), (size_hbm, size_ref))
    ):
        smalls.append(pltpu.make_async_copy(there, here, small_sem.at[n]))
        smalls[-1].start()
    parts = (x, 1 - x)
    table_in = []
    for n, part in enumerate(parts):
        table_in.append(
            pltpu.make_async_copy(el_ref.at[pl.ds(h * rows, rows), part], table.at[n], tab_sem.at[n])
        )
        table_in[-1].start()

    barrier = pltpu.get_barrier_semaphore()
    for m in range(1, n_src):
        pl.semaphore_signal(barrier, 1, device_id=(flipped(s, m), c), device_id_type=MESH)
    for m in range(1, 4):
        pl.semaphore_signal(barrier, 1, device_id=(s, flipped(c, m)), device_id_type=MESH)

    def tau_part(owner):
        return tau_ref.at[:, 0, pl.ds(owner * times, times)]

    tau_in = pltpu.make_async_copy(tau_part(x), xbuf.at[:, :, c], tau_own)
    tau_in.start()

    sub = lax.broadcasted_iota(jnp.int32, (n_ids, ne), 0)
    lane = lax.broadcasted_iota(jnp.int32, (n_ids, ne), 1)
    smalls[0].wait()

    def one_hot(owners):
        hots = []
        for i in owners:
            wanted = jnp.zeros((n_ids, ne), jnp.int32)
            for k in range(n_ids):
                wanted = jnp.where(sub == k, ids_ref[i, k], wanted)
            hots.append((wanted == lane).astype(f32))
        return jnp.concatenate(hots, axis=0).astype(bf16)

    def pick_rows(n, hot, target):
        count = target.shape[0] * n_ids
        for r in range(rows):
            got = lax.dot_general(hot, table[n, r], NN, preferred_element_type=f32)
            for side in range(nv // 128):
                pick[side, pl.ds(r, count, stride=rows), :] = got[:, side * 128:(side + 1) * 128]
        for i in range(target.shape[0]):
            for side in range(nv // 128):
                target[i, :, :, side * 128:(side + 1) * 128] = (
                    pick[side, pl.ds(i * n_ids * rows, n_ids * rows), :]
                    .astype(bf16)
                    .reshape(n_ids, rows, 128)
                )

    def remote(src, dst, send, recv, device):
        return pltpu.make_async_remote_copy(
            src_ref=src, dst_ref=dst, send_sem=send, recv_sem=recv,
            device_id=device, device_id_type=MESH,
        )

    started = []

    def go(copy):
        copy.start()
        started.append(copy)
        return copy

    def place(kind, part, source):
        return source_rows.at[part, h, source] if kind == 0 else sink_rows.at[part, source]

    hot = one_hot(range(n_src))
    table_in[0].wait()
    pick_rows(0, hot, sendbuf)

    depth, lane_y = s // 2, s % 2
    inner = ((depth + 1) // 2) % 2
    other_half = 1 - depth // 2
    inner_at, outer_at = 1 + other_half, 3 * other_half

    far = []
    for kind in (0, 1):
        for y_flip in (0, 1):
            for n, there in ((1, outer_at), (0, inner_at)):
                peer = there * 2 + flipped(lane_y, y_flip)
                far.append(remote(
                    sendbuf.at[peer, ids_of[kind]], place(kind, x, s),
                    far_send.at[kind, 2 * n + y_flip], far_recv.at[kind, 2 * (1 - inner) + y_flip],
                    (peer, c),
                ))

    direct = {}

    def send_direct(n, chunk_of):
        for kind in (0, 1):
            for m in (2, 3, 1):
                direct[n, kind, m] = remote(
                    chunk_of(flipped(s, m)).at[ids_of[kind]], place(kind, parts[n], s),
                    direct_send.at[n, kind, m], direct_recv.at[n, kind, m], (flipped(s, m), c),
                )
                go(direct[n, kind, m])

    own = {}

    def keep_own(n, chunk):
        for kind in (0, 1):
            own[n, kind] = pltpu.make_async_copy(
                chunk.at[ids_of[kind]], place(kind, parts[n], s), own_sem.at[n, kind]
            )
            own[n, kind].start()

    pl.semaphore_wait(barrier, n_src - 1 + 3)

    tau_out = {}

    def send_tau(m, owner):
        tau_out[m] = go(remote(
            tau_part(owner), xbuf.at[:, :, c], tau_send.at[m], tau_recv.at[m], (s, flipped(c, m)),
        ))

    for copy in far[:HALF]:
        copy.start()
    send_tau(2, 1 - x)
    send_direct(0, lambda i: sendbuf.at[i])
    send_tau(1, x)
    keep_own(0, sendbuf.at[s])
    table_in[1].wait()
    pick_rows(1, one_hot([base + i for i in range(HALF)]), sendother)
    send_direct(1, lambda i: sendother.at[i - base])
    keep_own(1, sendother.at[s - base])

    def far_source(q):
        return (inner_at, outer_at)[q // 2] * 2 + flipped(lane_y, q % 2)

    near_in = []

    def to_near(ref, at):
        near_in.append(go(remote(ref, ref, near_send.at[at], near_recv.at[at], (s, near))))

    def pass_half(n):
        own[n, 0].wait()
        for m in (1, 2, 3):
            direct[n, 0, m].wait_recv()
        to_near(source_rows.at[parts[n], h, pl.ds(base, HALF)], n)

    relayed = {}

    def relay(kind, q):
        chunk = place(kind, x, far_source(q))
        remote(chunk, chunk, on_send.at[kind, q], far_recv.at[kind, q], (s, across)).wait_recv()
        relayed[kind, q] = go(remote(
            chunk, chunk, on_send.at[kind, q], on_recv.at[kind, q], (s, across)
        ))
        if kind == 0:
            to_near(chunk, 2 + q)

    def pass_on(q):
        relayed[0, q].wait_recv()
        to_near(place(0, 1 - x, far_source(q)), 6 + q)

    def pass_tau():
        tau_out[2].wait_recv()
        theirs = xbuf.at[:, :, across]
        tau_out[3] = go(remote(theirs, theirs, tau_pass_send, tau_pass_recv, (s, near)))

    def turn_tau():
        tau_in.wait()
        tau_out[1].wait_recv()
        tau_out[3].wait_recv()
        blocks = nv // rows

        def one(t, carry):
            for part in (0, 1):
                spun[part] = jnp.transpose(xbuf[part, t].reshape(nv, nv)).reshape(blocks, rows, nv)
            for i in range(n_src):
                down = slice(i * rows, (i + 1) * rows)
                re, im = spun[0, 2 * i + h], spun[1, 2 * i + h]
                turned[0, t, 0, down] = re
                turned[0, t, 1, down] = -im
                turned[1, t, 0, down] = im
                turned[1, t, 1, down] = re
            return carry

        lax.fori_loop(0, times, one, 0)

    def mm(a, b, dims):
        return lax.dot_general(a, b, dims, preferred_element_type=f32)

    def stacked(part, k):
        return jnp.concatenate(
            [source_rows[part, side, i, k] for i in range(n_src) for side in range(2)], axis=0
        )

    mid = nv // 2

    def rights(k, carry):
        e_re, e_im = stacked(0, k), stacked(1, k)
        for t in range(times):
            got = (
                mm(turned[0, t].reshape(nv, nv), e_re, NT) + mm(turned[1, t].reshape(nv, nv), e_im, NT)
            ).astype(bf16)
            right_pos[t, k, 0] = got[:mid]
            right_pos[t, k, 1] = got[mid:]
            right_neg[t, k, 0] = -got[mid:]
            right_neg[t, k, 1] = got[:mid]
        return carry

    def wholes(t, carry):
        x_re, x_im = xbuf[0, t].reshape(nv, nv), xbuf[1, t].reshape(nv, nv)
        for k in range(n_source):
            got = mm(right_pos[t, k].reshape(nv, nv), x_re, NN) + mm(
                right_neg[t, k].reshape(nv, nv), x_im, NN
            )
            xmat[t, k, 0] = got[:mid]
            xmat[t, k, 1] = got[mid:]
        return carry

    n_diag = diag_ref.shape[2]
    zero = jnp.zeros((8, 128), f32)

    def products(sources, first):
        for n, i in enumerate(sources):
            for part in (0, 1):
                for k in range(n_sink):
                    staged[n, part, k] = sink_rows[part, i, k].astype(f32)

        def one(d, carry):
            k1, k2 = diag_ref[0, 0, d], diag_ref[1, 0, d]
            acc = [zero if first else sums[d, n] for n in range(2 * times)]
            for n, i in enumerate(sources):
                e_re, e_im = staged[n, 0, k1], staged[n, 1, k1]
                down = pl.ds(pl.multiple_of(i * rows, rows), rows)
                for t in range(times):
                    x_re, x_im = xmat[t, k2, 0, down, :], xmat[t, k2, 1, down, :]
                    re = e_re * x_re - e_im * x_im
                    im = e_re * x_im + e_im * x_re
                    for m, value in ((2 * t, re), (2 * t + 1, im)):
                        for r in range(rows // 8):
                            for l in range(nv // 128):
                                acc[m] = acc[m] + value[r * 8:(r + 1) * 8, l * 128:(l + 1) * 128]
            for n in range(2 * times):
                sums[d, n] = acc[n]
            return carry

        lax.fori_loop(0, n_diag, one, 0)

    for n, q in enumerate((2, 3, 0, 1)):
        far[n].wait_send()
        far[HALF + n].start()
        relay(0, q)
    pass_on(2)
    pass_on(3)
    pass_half(0)
    pass_tau()
    pass_on(0)
    pass_half(1)
    pass_on(1)
    turn_tau()
    relay(1, 0)
    for copy in near_in:
        copy.wait_recv()
    lax.fori_loop(0, n_source // 2, rights, 0)
    relay(1, 1)
    relay(1, 2)
    lax.fori_loop(n_source // 2, n_source, rights, 0)
    wholes(0, 0)
    relay(1, 3)
    lax.fori_loop(1, times, wholes, 0)

    for copy in smalls[1:]:
        copy.wait()
    for n in (0, 1):
        own[n, 1].wait()
        for m in (1, 2, 3):
            direct[n, 1, m].wait_recv()
    products([base + i for i in range(HALF)], True)
    for q in range(HALF):
        relayed[1, q].wait_recv()
        products([far_source(q)], False)

    values = []
    for t in range(times):
        real, imag = [], []
        for d in range(n_diag):
            turn = phase_ref[diag_ref[2, 0, d]]
            cosine = (turn == 0).astype(f32) - (turn == 2).astype(f32)
            sine = (turn == 1).astype(f32) - (turn == 3).astype(f32)
            re = jnp.sum(sums[d, 2 * t], axis=0, keepdims=True)
            im = jnp.sum(sums[d, 2 * t + 1], axis=0, keepdims=True)
            real.append(cosine * re - sine * im)
            imag.append(sine * re + cosine * im)
        values += real + imag
    flat = jnp.sum(jnp.transpose(jnp.concatenate(values, axis=0)), axis=0, keepdims=True)
    width = 2 * n_diag
    sub8 = lax.broadcasted_iota(jnp.int32, (8, width), 0)
    tile = jnp.zeros((8, width), f32)
    for t in range(times):
        tile = jnp.where(sub8 == x * times + t, flat[:, t * width:(t + 1) * width], tile)
    vbuf[c, :, :width] = tile

    val_out = []
    for m in (2, 3, 1):
        val_out.append(go(remote(
            vbuf.at[c], vbuf.at[c], val_send.at[m], val_recv.at[m], (s, flipped(c, m)),
        )))
    for copy in val_out:
        copy.wait_recv()

    whole = vbuf[0, :, :width]
    for n in range(1, vbuf.shape[0]):
        whole = whole + vbuf[n, :, :width]
    total[:, :width] = whole
    first, size = 0, 0
    for j in range(size_ref.shape[0]):
        first = first + jnp.where(j < c, size_ref[j], 0)
        size = size + jnp.where(j == c, size_ref[j], 0)
    for at_place in range(MAXB):
        at = jnp.minimum(first + at_place, total.shape[0] - 1)
        keep = (at_place < size).astype(f32)
        row = total[pl.ds(at, 1), :width] * keep
        out_ref[at_place, 0:1, :] = row[:, :n_diag]
        out_ref[at_place, 1:2, :] = row[:, n_diag:]

    for copy in far[HALF:] + started:
        copy.wait_send()


def fused_local(tau_cols, elementals, need_ids, diagrams, phases, block_sizes):
    n_snk = lax.axis_size("snk")
    n_src, n_ids = need_ids.shape
    own_rows, _, ne, nv = elementals.shape
    sinks, cols = tau_cols.shape[2], tau_cols.shape[3]
    times = sinks // 2
    rows = own_rows // 2
    n_diag = diagrams.shape[1]
    n_right = n_ids - NSN
    bf16, f32 = jnp.bfloat16, jnp.float32
    sem = pltpu.SemaphoreType.DMA
    i32 = jnp.int32
    held = pl.BlockSpec(memory_space=pltpu.HBM)
    values = pl.pallas_call(
        kernel,
        out_shape=jax.ShapeDtypeStruct((MAXB, 2, n_diag), f32),
        in_specs=[held] * 6,
        out_specs=pl.BlockSpec(memory_space=pltpu.VMEM),
        scratch_shapes=[
            pltpu.SMEM((n_src, n_ids), i32),
            pltpu.SMEM((3, 1, n_diag), i32),
            pltpu.SMEM(phases.shape, i32),
            pltpu.SMEM(block_sizes.shape, i32),
            pltpu.VMEM((2, rows, ne, nv), bf16),
            pltpu.VMEM((nv // 128, n_src * n_ids * rows, 128), f32),
            pltpu.VMEM((n_src, n_ids, rows, nv), bf16),
            pltpu.VMEM((HALF, n_ids, rows, nv), bf16),
            pltpu.VMEM((2, n_src, NSN, rows, nv), bf16),
            pltpu.VMEM((2, 2, n_src, n_right, rows, nv), bf16),
            pltpu.VMEM((2, times, n_snk, cols, nv), bf16),
            pltpu.VMEM((2, nv // rows, rows, nv), bf16),
            pltpu.VMEM((2, times, 2, nv // 2, nv), bf16),
            pltpu.VMEM((times, n_right, 2, nv // 2, nv), bf16),
            pltpu.VMEM((times, n_right, 2, nv // 2, nv), bf16),
            pltpu.VMEM((times, n_right, 2, nv // 2, nv), f32),
            pltpu.VMEM((HALF, 2, NSN, rows, nv), f32),
            pltpu.VMEM((n_diag, 2 * times, 8, 128), f32),
            pltpu.VMEM((n_snk, 8, 128), f32),
            pltpu.VMEM((8, 128), f32),
            sem((4,)), sem((2,)), sem((2, 2)), sem, sem((4,)), sem((4,)), sem, sem,
            sem((2, 2, 4)), sem((2, 2, 4)), sem((2, 4)), sem((2, 4)), sem((2, 4)), sem((2, 4)),
            sem((10,)), sem((10,)), sem((4,)), sem((4,)),
        ],
        compiler_params=pltpu.CompilerParams(
            collective_id=0, has_side_effects=True, vmem_limit_bytes=67043328
        ),
    )(need_ids, jnp.transpose(diagrams, (2, 0, 1)), phases, block_sizes, tau_cols, elementals)
    return values.reshape(1, 1, MAXB, 2, n_diag)


def local(tau_cols, elementals, *rest):
    fits = (
        lax.axis_size("snk") == 4
        and lax.axis_size("src") == 8
        and elementals.shape[0] == 32
        and tau_cols.shape[2] == 8
        and tau_cols.shape[3] == 64
        and tau_cols.shape[4] == 256
    )
    return (fused_local if fits else plain_local)(tau_cols, elementals, *rest)


def solution(mesh):
    placed = (
        P(None, "src", None, "snk", None),
        P("src", None, None, None),
        P(),
        P("src", None, None),
        P(),
        P(),
    )
    return jax.shard_map(
        local,
        mesh=mesh,
        in_specs=placed,
        out_specs=P("src", "snk", None, None, None),
        check_vma=False,
    )
```

```python
import functools

import jax
import jax.numpy as jnp
from jax import lax
from jax.experimental import pallas as pl
from jax.experimental.pallas import tpu as pltpu
from jax.sharding import PartitionSpec as P

NSN = 4
MAXB = 3


def slot_values(gathered, tau_slot, diagram_rows, phases):
    real_part = tau_slot[0]
    imag_part = tau_slot[1]
    left_stack = jnp.stack([jnp.stack([real_part, imag_part]), jnp.stack([-imag_part, real_part])])
    right_stack = jnp.stack([jnp.stack([real_part, -imag_part]), jnp.stack([imag_part, real_part])])
    left_node = lax.dot_general(
        gathered[:, :, :NSN],
        left_stack,
        (((1, 3), (0, 3)), ((), ())),
        preferred_element_type=jnp.float32,
    ).astype(jnp.bfloat16)
    right_node = lax.dot_general(
        gathered[:, :, NSN:],
        right_stack,
        (((1, 3), (0, 2)), ((), ())),
        preferred_element_type=jnp.float32,
    ).astype(jnp.bfloat16)
    pair_sums = lax.dot_general(
        left_node, right_node, (((0, 3), (3, 0)), ((), ())), preferred_element_type=jnp.float32
    )
    pair_real = pair_sums[:, 0, :, 0] - pair_sums[:, 1, :, 1]
    pair_imag = pair_sums[:, 0, :, 1] + pair_sums[:, 1, :, 0]
    sink_pick = (
        diagram_rows[:, 0:1] == jnp.arange(pair_real.shape[0], dtype=jnp.int32)[None, :]
    ).astype(jnp.float32)
    source_pick = (
        diagram_rows[:, 1:2] == jnp.arange(pair_real.shape[1], dtype=jnp.int32)[None, :]
    ).astype(jnp.float32)
    chosen_real = jnp.sum(
        sink_pick[:, :, None] * pair_real[None] * source_pick[:, None, :], axis=(1, 2)
    )
    chosen_imag = jnp.sum(
        sink_pick[:, :, None] * pair_imag[None] * source_pick[:, None, :], axis=(1, 2)
    )
    gamma_pick = diagram_rows[:, 2:3] == jnp.arange(phases.shape[0], dtype=jnp.int32)[None, :]
    quarter = jnp.sum(jnp.where(gamma_pick, phases[None, :], 0), axis=1)
    cosine = (quarter == 0).astype(jnp.float32) - (quarter == 2).astype(jnp.float32)
    sine_part = (quarter == 1).astype(jnp.float32) - (quarter == 3).astype(jnp.float32)
    return jnp.stack(
        [
            cosine * chosen_real - sine_part * chosen_imag,
            sine_part * chosen_real + cosine * chosen_imag,
        ]
    )


def plain_local(tau_cols, elementals, need_ids, diagrams, phases, block_sizes):
    groups = lax.axis_size("snk")
    column = lax.axis_index("snk")
    full_width = tau_cols.shape[4]
    col_count = tau_cols.shape[3]
    sink_count = tau_cols.shape[2]
    diagram_rows = diagrams[0]
    block_at = jnp.arange(block_sizes.shape[0], dtype=jnp.int32)
    starts = jnp.sum(
        jnp.where(block_at[None, :] < block_at[:, None], block_sizes[None, :], 0), axis=1
    )
    offsets = jnp.arange(MAXB, dtype=jnp.int32)
    picked = jnp.take(elementals, need_ids, axis=2)
    arrived = lax.all_to_all(picked, "src", split_axis=2, concat_axis=0, tiled=True)
    gathered = arrived.reshape(full_width, 2, need_ids.shape[1], full_width)
    local_tau = tau_cols[:, 0]
    per_group = sink_count // groups
    half_turn = groups // 2
    packed = local_tau.reshape(2, groups, per_group, col_count, full_width)
    packed = jnp.roll(packed, -half_turn, axis=1)
    arrived_tau = lax.all_to_all(packed, "snk", split_axis=1, concat_axis=3, tiled=True)
    blocks = arrived_tau.reshape(2, per_group, full_width, full_width)
    results = jnp.stack(
        [
            slot_values(gathered, blocks[:, place], diagram_rows, phases)
            for place in range(per_group)
        ]
    )
    all_values = lax.all_gather(results, "snk", axis=0, tiled=True)
    all_values = jnp.roll(all_values, half_turn * per_group, axis=0)
    own_start = lax.dynamic_index_in_dim(starts, column, keepdims=False)
    own_size = lax.dynamic_index_in_dim(block_sizes, column, keepdims=False)
    own_filled = offsets < own_size
    own_times = jnp.where(own_filled, own_start + offsets, 0)
    wanted = own_filled[:, None] & (
        own_times[:, None] == jnp.arange(all_values.shape[0], dtype=jnp.int32)[None, :]
    )
    correlators = jnp.sum(jnp.where(wanted[:, :, None, None], all_values[None], 0.0), axis=1)
    return correlators.reshape(1, 1, MAXB, 2, diagram_rows.shape[0])


MESH = pl.DeviceIdType.MESH
HALF = 4
PIECES = 2
NT = (((1,), (1,)), ((), ()))
NN = (((1,), (0,)), ((), ()))


def flipped(value, mask):
    for bit in (1, 2, 4):
        if mask & bit:
            value = value + bit * (1 - 2 * ((value // bit) % 2))
    return value


def kernel(
    ids_hbm, diag_hbm, phase_hbm, size_hbm, tau_ref, el_ref, out_ref,
    ids_ref, diag_ref, phase_ref, size_ref,
    table, pick, sendbuf, sendother, sink_rows, source_rows, xbuf,
    spun, turned, right_pos, right_neg, xmat, staged, sums, vbuf, total,
    small_sem, tab_sem, own_sem, tau_own, tau_send, tau_recv, tau_pass_send, tau_pass_recv,
    direct_send, direct_recv, far_send, far_recv, on_send, on_recv, near_send, near_recv,
    val_send, val_recv,
):
    s = lax.axis_index("src")
    c = lax.axis_index("snk")
    x, h = c // 2, c % 2
    n_src, n_ids = ids_ref.shape
    rows, ne, nv = table.shape[1:]
    times = xbuf.shape[1]
    f32, bf16 = jnp.float32, jnp.bfloat16
    base = (s // HALF) * HALF
    near, across = flipped(c, 1), flipped(c, 2)
    n_sink, n_source = sink_rows.shape[2], source_rows.shape[3]
    ids_of = (pl.ds(n_sink, n_source), pl.ds(0, n_sink))

    smalls = []
    for n, (there, here) in enumerate(
        ((ids_hbm, ids_ref), (diag_hbm, diag_ref), (phase_hbm, phase_ref), (size_hbm, size_ref))
    ):
        smalls.append(pltpu.make_async_copy(there, here, small_sem.at[n]))
        smalls[-1].start()
    parts = (x, 1 - x)
    table_in = []
    for n, part in enumerate(parts):
        table_in.append([])
        for piece in range(PIECES):
            step = rows // PIECES
            table_in[n].append(
                pltpu.make_async_copy(
                    el_ref.at[pl.ds(h * rows + piece * step, step), part],
                    table.at[n, pl.ds(piece * step, step)], tab_sem.at[n, piece],
                )
            )
            table_in[n][piece].start()

    barrier = pltpu.get_barrier_semaphore()
    for m in range(1, n_src):
        pl.semaphore_signal(barrier, 1, device_id=(flipped(s, m), c), device_id_type=MESH)
    for m in range(1, 4):
        pl.semaphore_signal(barrier, 1, device_id=(s, flipped(c, m)), device_id_type=MESH)

    def tau_part(owner):
        return tau_ref.at[:, 0, pl.ds(owner * times, times)]

    tau_in = pltpu.make_async_copy(tau_part(x), xbuf.at[:, :, c], tau_own)
    tau_in.start()

    sub = lax.broadcasted_iota(jnp.int32, (n_ids, ne), 0)
    lane = lax.broadcasted_iota(jnp.int32, (n_ids, ne), 1)
    smalls[0].wait()

    def one_hot(owners):
        hots = []
        for i in owners:
            wanted = jnp.zeros((n_ids, ne), jnp.int32)
            for k in range(n_ids):
                wanted = jnp.where(sub == k, ids_ref[i, k], wanted)
            hots.append((wanted == lane).astype(f32))
        return jnp.concatenate(hots, axis=0).astype(bf16)

    def pick_rows(n, hot, target):
        count = target.shape[0] * n_ids
        for r in range(rows):
            if r % (rows // PIECES) == 0:
                table_in[n][r // (rows // PIECES)].wait()
            got = lax.dot_general(hot, table[n, r], NN, preferred_element_type=f32)
            for side in range(nv // 128):
                pick[side, pl.ds(r, count, stride=rows), :] = got[:, side * 128:(side + 1) * 128]
        for i in range(target.shape[0]):
            for side in range(nv // 128):
                target[i, :, :, side * 128:(side + 1) * 128] = (
                    pick[side, pl.ds(i * n_ids * rows, n_ids * rows), :]
                    .astype(bf16)
                    .reshape(n_ids, rows, 128)
                )

    def remote(src, dst, send, recv, device):
        return pltpu.make_async_remote_copy(
            src_ref=src, dst_ref=dst, send_sem=send, recv_sem=recv,
            device_id=device, device_id_type=MESH,
        )

    started = []

    def go(copy):
        copy.start()
        started.append(copy)
        return copy

    def place(kind, part, source):
        return source_rows.at[part, h, source] if kind == 0 else sink_rows.at[part, source]

    hot = one_hot(range(n_src))
    pick_rows(0, hot, sendbuf)

    depth, lane_y = s // 2, s % 2
    inner = ((depth + 1) // 2) % 2
    other_half = 1 - depth // 2
    inner_at, outer_at = 1 + other_half, 3 * other_half

    far = []
    for kind in (0, 1):
        for y_flip in (0, 1):
            for n, there in ((1, outer_at), (0, inner_at)):
                peer = there * 2 + flipped(lane_y, y_flip)
                far.append(remote(
                    sendbuf.at[peer, ids_of[kind]], place(kind, x, s),
                    far_send.at[kind, 2 * n + y_flip], far_recv.at[kind, 2 * (1 - inner) + y_flip],
                    (peer, c),
                ))

    direct = {}

    def send_direct(n, chunk_of):
        for kind in (0, 1):
            for m in (2, 3, 1):
                direct[n, kind, m] = remote(
                    chunk_of(flipped(s, m)).at[ids_of[kind]], place(kind, parts[n], s),
                    direct_send.at[n, kind, m], direct_recv.at[n, kind, m], (flipped(s, m), c),
                )
                go(direct[n, kind, m])

    own = {}

    def keep_own(n, chunk):
        for kind in (0, 1):
            own[n, kind] = pltpu.make_async_copy(
                chunk.at[ids_of[kind]], place(kind, parts[n], s), own_sem.at[n, kind]
            )
            own[n, kind].start()

    pl.semaphore_wait(barrier, n_src - 1 + 3)

    tau_out = {}

    def send_tau(m, owner):
        tau_out[m] = go(remote(
            tau_part(owner), xbuf.at[:, :, c], tau_send.at[m], tau_recv.at[m], (s, flipped(c, m)),
        ))

    for copy in far[:HALF]:
        copy.start()
    send_tau(2, 1 - x)
    send_direct(0, lambda i: sendbuf.at[i])
    send_tau(1, x)
    keep_own(0, sendbuf.at[s])
    pick_rows(1, one_hot([base + i for i in range(HALF)]), sendother)
    send_direct(1, lambda i: sendother.at[i - base])
    keep_own(1, sendother.at[s - base])

    def far_source(q):
        return (inner_at, outer_at)[q // 2] * 2 + flipped(lane_y, q % 2)

    near_in = []

    def to_near(ref, at):
        near_in.append(go(remote(ref, ref, near_send.at[at], near_recv.at[at], (s, near))))

    def pass_half(n):
        own[n, 0].wait()
        for m in (1, 2, 3):
            direct[n, 0, m].wait_recv()
        to_near(source_rows.at[parts[n], h, pl.ds(base, HALF)], n)

    relayed = {}

    def relay(kind, q):
        chunk = place(kind, x, far_source(q))
        remote(chunk, chunk, on_send.at[kind, q], far_recv.at[kind, q], (s, across)).wait_recv()
        relayed[kind, q] = go(remote(
            chunk, chunk, on_send.at[kind, q], on_recv.at[kind, q], (s, across)
        ))
        if kind == 0:
            to_near(chunk, 2 + q)

    def pass_on(q):
        relayed[0, q].wait_recv()
        to_near(place(0, 1 - x, far_source(q)), 6 + q)

    def pass_tau():
        tau_out[2].wait_recv()
        theirs = xbuf.at[:, :, across]
        tau_out[3] = go(remote(theirs, theirs, tau_pass_send, tau_pass_recv, (s, near)))

    def turn_tau():
        tau_in.wait()
        tau_out[1].wait_recv()
        tau_out[3].wait_recv()
        blocks = nv // rows

        def one(t, carry):
            for part in (0, 1):
                spun[part] = jnp.transpose(xbuf[part, t].reshape(nv, nv)).reshape(blocks, rows, nv)
            for i in range(n_src):
                down = slice(i * rows, (i + 1) * rows)
                re, im = spun[0, 2 * i + h], spun[1, 2 * i + h]
                turned[0, t, 0, down] = re
                turned[0, t, 1, down] = -im
                turned[1, t, 0, down] = im
                turned[1, t, 1, down] = re
            return carry

        lax.fori_loop(0, times, one, 0)

    def mm(a, b, dims):
        return lax.dot_general(a, b, dims, preferred_element_type=f32)

    def stacked(part, k):
        return jnp.concatenate(
            [source_rows[part, side, i, k] for i in range(n_src) for side in range(2)], axis=0
        )

    mid = nv // 2

    def rights(k, carry):
        e_re, e_im = stacked(0, k), stacked(1, k)
        for t in range(times):
            got = (
                mm(turned[0, t].reshape(nv, nv), e_re, NT) + mm(turned[1, t].reshape(nv, nv), e_im, NT)
            ).astype(bf16)
            right_pos[t, k, 0] = got[:mid]
            right_pos[t, k, 1] = got[mid:]
            right_neg[t, k, 0] = -got[mid:]
            right_neg[t, k, 1] = got[:mid]
        return carry

    def wholes(t, carry):
        x_re, x_im = xbuf[0, t].reshape(nv, nv), xbuf[1, t].reshape(nv, nv)
        for k in range(n_source):
            got = mm(right_pos[t, k].reshape(nv, nv), x_re, NN) + mm(
                right_neg[t, k].reshape(nv, nv), x_im, NN
            )
            xmat[t, k, 0] = got[:mid]
            xmat[t, k, 1] = got[mid:]
        return carry

    n_diag = diag_ref.shape[2]
    zero = jnp.zeros((8, 128), f32)

    def products(sources, first):
        for n, i in enumerate(sources):
            for part in (0, 1):
                for k in range(n_sink):
                    staged[n, part, k] = sink_rows[part, i, k].astype(f32)

        def one(d, carry):
            k1, k2 = diag_ref[0, 0, d], diag_ref[1, 0, d]
            acc = [zero if first else sums[d, n] for n in range(2 * times)]
            for n, i in enumerate(sources):
                e_re, e_im = staged[n, 0, k1], staged[n, 1, k1]
                down = pl.ds(pl.multiple_of(i * rows, rows), rows)
                for t in range(times):
                    x_re, x_im = xmat[t, k2, 0, down, :], xmat[t, k2, 1, down, :]
                    re = e_re * x_re - e_im * x_im
                    im = e_re * x_im + e_im * x_re
                    for m, value in ((2 * t, re), (2 * t + 1, im)):
                        for r in range(rows // 8):
                            for l in range(nv // 128):
                                acc[m] = acc[m] + value[r * 8:(r + 1) * 8, l * 128:(l + 1) * 128]
            for n in range(2 * times):
                sums[d, n] = acc[n]
            return carry

        lax.fori_loop(0, n_diag, one, 0)

    for n, q in enumerate((2, 3, 0, 1)):
        far[n].wait_send()
        far[HALF + n].start()
        relay(0, q)
    pass_on(2)
    pass_on(3)
    pass_half(0)
    pass_tau()
    pass_on(0)
    pass_half(1)
    pass_on(1)
    turn_tau()
    relay(1, 0)
    for copy in near_in:
        copy.wait_recv()
    lax.fori_loop(0, n_source // 2, rights, 0)
    relay(1, 1)
    relay(1, 2)
    lax.fori_loop(n_source // 2, n_source, rights, 0)
    wholes(0, 0)
    relay(1, 3)
    lax.fori_loop(1, times, wholes, 0)

    for copy in smalls[1:]:
        copy.wait()
    for n in (0, 1):
        own[n, 1].wait()
        for m in (1, 2, 3):
            direct[n, 1, m].wait_recv()
    width = 2 * n_diag
    sub8 = lax.broadcasted_iota(jnp.int32, (8, width), 0)
    lane8 = lax.broadcasted_iota(jnp.int32, (8, width), 1)
    cosine, sine = jnp.zeros((8, width), f32), jnp.zeros((8, width), f32)
    for d in range(n_diag):
        turn = phase_ref[diag_ref[2, 0, d]]
        cos_d = (turn == 0).astype(f32) - (turn == 2).astype(f32)
        sin_d = (turn == 1).astype(f32) - (turn == 3).astype(f32)
        cosine = jnp.where(lane8 % n_diag == d, cos_d, cosine)
        sine = jnp.where(lane8 == d, -sin_d, jnp.where(lane8 == n_diag + d, sin_d, sine))
    first, size = 0, 0
    for j in range(size_ref.shape[0]):
        first = first + jnp.where(j < c, size_ref[j], 0)
        size = size + jnp.where(j == c, size_ref[j], 0)
    products([base + i for i in range(HALF)], True)
    for q in range(HALF):
        relayed[1, q].wait_recv()
        products([far_source(q)], False)

    flat = jnp.concatenate(
        [
            jnp.sum(sums[d, 2 * t + n], axis=0, keepdims=True)
            for t in range(times) for n in (0, 1) for d in range(n_diag)
        ],
        axis=0,
    )
    flat = jnp.sum(jnp.transpose(flat), axis=0, keepdims=True)
    tile = jnp.zeros((8, width), f32)
    for t in range(times):
        tile = jnp.where(sub8 == x * times + t, flat[:, t * width:(t + 1) * width], tile)
    vbuf[c, :, :width] = tile

    val_out = []
    for m in (2, 3, 1):
        val_out.append(go(remote(
            vbuf.at[c], vbuf.at[c], val_send.at[m], val_recv.at[m], (s, flipped(c, m)),
        )))
    for copy in val_out:
        copy.wait_recv()

    whole = vbuf[0, :, :width]
    for n in range(1, vbuf.shape[0]):
        whole = whole + vbuf[n, :, :width]
    swapped = jnp.concatenate([whole[:, n_diag:], whole[:, :n_diag]], axis=1)
    total[:, :width] = cosine * whole + sine * swapped
    for at_place in range(MAXB):
        at = jnp.minimum(first + at_place, total.shape[0] - 1)
        keep = (at_place < size).astype(f32)
        row = total[pl.ds(at, 1), :width] * keep
        out_ref[at_place, 0:1, :] = row[:, :n_diag]
        out_ref[at_place, 1:2, :] = row[:, n_diag:]

    for copy in far[HALF:] + started:
        copy.wait_send()


def fused_local(tau_cols, elementals, need_ids, diagrams, phases, block_sizes):
    n_snk = lax.axis_size("snk")
    n_src, n_ids = need_ids.shape
    own_rows, _, ne, nv = elementals.shape
    sinks, cols = tau_cols.shape[2], tau_cols.shape[3]
    times = sinks // 2
    rows = own_rows // 2
    n_diag = diagrams.shape[1]
    n_right = n_ids - NSN
    bf16, f32 = jnp.bfloat16, jnp.float32
    sem = pltpu.SemaphoreType.DMA
    i32 = jnp.int32
    held = pl.BlockSpec(memory_space=pltpu.HBM)
    values = pl.pallas_call(
        kernel,
        out_shape=pltpu.VMEM((MAXB, 2, n_diag), f32),
        in_specs=[held] * 6,
        out_specs=pl.BlockSpec(memory_space=pltpu.VMEM),
        scratch_shapes=[
            pltpu.SMEM((n_src, n_ids), i32),
            pltpu.SMEM((3, 1, n_diag), i32),
            pltpu.SMEM(phases.shape, i32),
            pltpu.SMEM(block_sizes.shape, i32),
            pltpu.VMEM((2, rows, ne, nv), bf16),
            pltpu.VMEM((nv // 128, n_src * n_ids * rows, 128), f32),
            pltpu.VMEM((n_src, n_ids, rows, nv), bf16),
            pltpu.VMEM((HALF, n_ids, rows, nv), bf16),
            pltpu.VMEM((2, n_src, NSN, rows, nv), bf16),
            pltpu.VMEM((2, 2, n_src, n_right, rows, nv), bf16),
            pltpu.VMEM((2, times, n_snk, cols, nv), bf16),
            pltpu.VMEM((2, nv // rows, rows, nv), bf16),
            pltpu.VMEM((2, times, 2, nv // 2, nv), bf16),
            pltpu.VMEM((times, n_right, 2, nv // 2, nv), bf16),
            pltpu.VMEM((times, n_right, 2, nv // 2, nv), bf16),
            pltpu.VMEM((times, n_right, 2, nv // 2, nv), f32),
            pltpu.VMEM((HALF, 2, NSN, rows, nv), f32),
            pltpu.VMEM((n_diag, 2 * times, 8, 128), f32),
            pltpu.VMEM((n_snk, 8, 128), f32),
            pltpu.VMEM((8, 128), f32),
            sem((4,)), sem((2, PIECES)), sem((2, 2)), sem, sem((4,)), sem((4,)), sem, sem,
            sem((2, 2, 4)), sem((2, 2, 4)), sem((2, 4)), sem((2, 4)), sem((2, 4)), sem((2, 4)),
            sem((10,)), sem((10,)), sem((4,)), sem((4,)),
        ],
        compiler_params=pltpu.CompilerParams(
            collective_id=0, has_side_effects=True, vmem_limit_bytes=60 * 2**20
        ),
    )(need_ids, jnp.transpose(diagrams, (2, 0, 1)), phases, block_sizes, tau_cols, elementals)
    return values.reshape(1, 1, MAXB, 2, n_diag)


def local(tau_cols, elementals, *rest):
    fits = (
        lax.axis_size("snk") == 4
        and lax.axis_size("src") == 8
        and elementals.shape[0] == 32
        and tau_cols.shape[2] == 8
        and tau_cols.shape[3] == 64
        and tau_cols.shape[4] == 256
    )
    return (fused_local if fits else plain_local)(tau_cols, elementals, *rest)


def solution(mesh):
    placed = (
        P(None, "src", None, "snk", None),
        P("src", None, None, None),
        P(),
        P("src", None, None),
        P(),
        P(),
    )
    return jax.shard_map(
        local,
        mesh=mesh,
        in_specs=placed,
        out_specs=P("src", "snk", None, None, None),
        check_vma=False,
    )
```

```python
import functools

import jax
import jax.numpy as jnp
from jax import lax
from jax.experimental import pallas as pl
from jax.experimental.pallas import tpu as pltpu
from jax.sharding import PartitionSpec as P

NSN = 4
MAXB = 3


def slot_values(gathered, tau_slot, diagram_rows, phases):
    real_part = tau_slot[0]
    imag_part = tau_slot[1]
    left_stack = jnp.stack([jnp.stack([real_part, imag_part]), jnp.stack([-imag_part, real_part])])
    right_stack = jnp.stack([jnp.stack([real_part, -imag_part]), jnp.stack([imag_part, real_part])])
    left_node = lax.dot_general(
        gathered[:, :, :NSN],
        left_stack,
        (((1, 3), (0, 3)), ((), ())),
        preferred_element_type=jnp.float32,
    ).astype(jnp.bfloat16)
    right_node = lax.dot_general(
        gathered[:, :, NSN:],
        right_stack,
        (((1, 3), (0, 2)), ((), ())),
        preferred_element_type=jnp.float32,
    ).astype(jnp.bfloat16)
    pair_sums = lax.dot_general(
        left_node, right_node, (((0, 3), (3, 0)), ((), ())), preferred_element_type=jnp.float32
    )
    pair_real = pair_sums[:, 0, :, 0] - pair_sums[:, 1, :, 1]
    pair_imag = pair_sums[:, 0, :, 1] + pair_sums[:, 1, :, 0]
    sink_pick = (
        diagram_rows[:, 0:1] == jnp.arange(pair_real.shape[0], dtype=jnp.int32)[None, :]
    ).astype(jnp.float32)
    source_pick = (
        diagram_rows[:, 1:2] == jnp.arange(pair_real.shape[1], dtype=jnp.int32)[None, :]
    ).astype(jnp.float32)
    chosen_real = jnp.sum(
        sink_pick[:, :, None] * pair_real[None] * source_pick[:, None, :], axis=(1, 2)
    )
    chosen_imag = jnp.sum(
        sink_pick[:, :, None] * pair_imag[None] * source_pick[:, None, :], axis=(1, 2)
    )
    gamma_pick = diagram_rows[:, 2:3] == jnp.arange(phases.shape[0], dtype=jnp.int32)[None, :]
    quarter = jnp.sum(jnp.where(gamma_pick, phases[None, :], 0), axis=1)
    cosine = (quarter == 0).astype(jnp.float32) - (quarter == 2).astype(jnp.float32)
    sine_part = (quarter == 1).astype(jnp.float32) - (quarter == 3).astype(jnp.float32)
    return jnp.stack(
        [
            cosine * chosen_real - sine_part * chosen_imag,
            sine_part * chosen_real + cosine * chosen_imag,
        ]
    )


def plain_local(tau_cols, elementals, need_ids, diagrams, phases, block_sizes):
    groups = lax.axis_size("snk")
    column = lax.axis_index("snk")
    full_width = tau_cols.shape[4]
    col_count = tau_cols.shape[3]
    sink_count = tau_cols.shape[2]
    diagram_rows = diagrams[0]
    block_at = jnp.arange(block_sizes.shape[0], dtype=jnp.int32)
    starts = jnp.sum(
        jnp.where(block_at[None, :] < block_at[:, None], block_sizes[None, :], 0), axis=1
    )
    offsets = jnp.arange(MAXB, dtype=jnp.int32)
    picked = jnp.take(elementals, need_ids, axis=2)
    arrived = lax.all_to_all(picked, "src", split_axis=2, concat_axis=0, tiled=True)
    gathered = arrived.reshape(full_width, 2, need_ids.shape[1], full_width)
    local_tau = tau_cols[:, 0]
    per_group = sink_count // groups
    half_turn = groups // 2
    packed = local_tau.reshape(2, groups, per_group, col_count, full_width)
    packed = jnp.roll(packed, -half_turn, axis=1)
    arrived_tau = lax.all_to_all(packed, "snk", split_axis=1, concat_axis=3, tiled=True)
    blocks = arrived_tau.reshape(2, per_group, full_width, full_width)
    results = jnp.stack(
        [
            slot_values(gathered, blocks[:, place], diagram_rows, phases)
            for place in range(per_group)
        ]
    )
    all_values = lax.all_gather(results, "snk", axis=0, tiled=True)
    all_values = jnp.roll(all_values, half_turn * per_group, axis=0)
    own_start = lax.dynamic_index_in_dim(starts, column, keepdims=False)
    own_size = lax.dynamic_index_in_dim(block_sizes, column, keepdims=False)
    own_filled = offsets < own_size
    own_times = jnp.where(own_filled, own_start + offsets, 0)
    wanted = own_filled[:, None] & (
        own_times[:, None] == jnp.arange(all_values.shape[0], dtype=jnp.int32)[None, :]
    )
    correlators = jnp.sum(jnp.where(wanted[:, :, None, None], all_values[None], 0.0), axis=1)
    return correlators.reshape(1, 1, MAXB, 2, diagram_rows.shape[0])


MESH = pl.DeviceIdType.MESH
HALF = 4
PIECES = 2
NT = (((1,), (1,)), ((), ()))
NN = (((1,), (0,)), ((), ()))


def flipped(value, mask):
    for bit in (1, 2, 4):
        if mask & bit:
            value = value + bit * (1 - 2 * ((value // bit) % 2))
    return value


def kernel(
    ids_hbm, diag_hbm, phase_hbm, size_hbm, tau_ref, el_ref, out_ref,
    ids_ref, diag_ref, phase_ref, size_ref,
    table, pick, sendbuf, sendother, sink_rows, source_rows, xbuf,
    spun, turned, right_pos, right_neg, xmat, staged, sums, vbuf, total,
    small_sem, tab_sem, own_sem, tau_own, tau_send, tau_recv, tau_pass_send, tau_pass_recv,
    direct_send, direct_recv, far_send, far_recv, on_send, on_recv, near_send, near_recv,
    val_send, val_recv,
):
    s = lax.axis_index("src")
    c = lax.axis_index("snk")
    x, h = c // 2, c % 2
    n_src, n_ids = ids_ref.shape
    rows, ne, nv = table.shape[1:]
    times = xbuf.shape[1]
    f32, bf16 = jnp.float32, jnp.bfloat16
    base = (s // HALF) * HALF
    near, across = flipped(c, 1), flipped(c, 2)
    n_sink, n_source = sink_rows.shape[2], source_rows.shape[3]
    ids_of = (pl.ds(n_sink, n_source), pl.ds(0, n_sink))

    smalls = []
    for n, (there, here) in enumerate(
        ((ids_hbm, ids_ref), (diag_hbm, diag_ref), (phase_hbm, phase_ref), (size_hbm, size_ref))
    ):
        smalls.append(pltpu.make_async_copy(there, here, small_sem.at[n]))
        smalls[-1].start()
    parts = (x, 1 - x)
    table_in = []
    for n, part in enumerate(parts):
        table_in.append([])
        for piece in range(PIECES):
            step = rows // PIECES
            table_in[n].append(
                pltpu.make_async_copy(
                    el_ref.at[pl.ds(h * rows + piece * step, step), part],
                    table.at[n, pl.ds(piece * step, step)], tab_sem.at[n, piece],
                )
            )
            table_in[n][piece].start()

    barrier = pltpu.get_barrier_semaphore()
    for m in range(1, n_src):
        pl.semaphore_signal(barrier, 1, device_id=(flipped(s, m), c), device_id_type=MESH)
    for m in range(1, 4):
        pl.semaphore_signal(barrier, 1, device_id=(s, flipped(c, m)), device_id_type=MESH)

    def tau_part(owner):
        return tau_ref.at[:, 0, pl.ds(owner * times, times)]

    tau_in = pltpu.make_async_copy(tau_part(x), xbuf.at[:, :, c], tau_own)
    tau_in.start()

    sub = lax.broadcasted_iota(jnp.int32, (n_ids, ne), 0)
    lane = lax.broadcasted_iota(jnp.int32, (n_ids, ne), 1)
    smalls[0].wait()

    def one_hot(owners):
        hots = []
        for i in owners:
            wanted = jnp.zeros((n_ids, ne), jnp.int32)
            for k in range(n_ids):
                wanted = jnp.where(sub == k, ids_ref[i, k], wanted)
            hots.append((wanted == lane).astype(f32))
        return jnp.concatenate(hots, axis=0).astype(bf16)

    def pick_rows(n, hot, count):
        for r in range(rows):
            if r % (rows // PIECES) == 0:
                table_in[n][r // (rows // PIECES)].wait()
            got = lax.dot_general(hot, table[n, r], NN, preferred_element_type=f32)
            for side in range(nv // 128):
                pick[side, pl.ds(r, count * n_ids, stride=rows), :] = got[:, side * 128:(side + 1) * 128]

    def lay_out(target, i, kind):
        first, count = (n_sink, n_source) if kind == 0 else (0, n_sink)
        down = pl.ds(pl.multiple_of((i * n_ids + first) * rows, rows), count * rows)
        for side in range(nv // 128):
            target[i, ids_of[kind], :, side * 128:(side + 1) * 128] = (
                pick[side, down, :].astype(bf16).reshape(count, rows, 128)
            )

    def remote(src, dst, send, recv, device):
        return pltpu.make_async_remote_copy(
            src_ref=src, dst_ref=dst, send_sem=send, recv_sem=recv,
            device_id=device, device_id_type=MESH,
        )

    started = []

    def go(copy):
        copy.start()
        started.append(copy)
        return copy

    def place(kind, part, source):
        return source_rows.at[part, h, source] if kind == 0 else sink_rows.at[part, source]

    away = HALF - base
    pick_rows(0, one_hot(range(n_src)), n_src)
    for i in range(HALF):
        lay_out(sendbuf, away + i, 0)

    depth, lane_y = s // 2, s % 2
    inner = ((depth + 1) // 2) % 2
    other_half = 1 - depth // 2
    inner_at, outer_at = 1 + other_half, 3 * other_half

    far = []
    for kind in (0, 1):
        for n, there, y in ((1, outer_at, 0), (0, inner_at, 0), (1, outer_at, 1), (0, inner_at, 1)):
            y_flip = (y + lane_y) % 2
            far.append(remote(
                sendbuf.at[there * 2 + y, ids_of[kind]], place(kind, x, s),
                far_send.at[kind, 2 * n + y], far_recv.at[kind, 2 * (1 - inner) + y_flip],
                (there * 2 + y, c),
            ))

    direct = {}

    def send_direct(n, chunk_of):
        for kind in (0, 1):
            for m in (2, 3, 1):
                direct[n, kind, m] = remote(
                    chunk_of(flipped(s, m)).at[ids_of[kind]], place(kind, parts[n], s),
                    direct_send.at[n, kind, m], direct_recv.at[n, kind, m], (flipped(s, m), c),
                )
                go(direct[n, kind, m])

    own = {}

    def keep_own(n, chunk):
        for kind in (0, 1):
            own[n, kind] = pltpu.make_async_copy(
                chunk.at[ids_of[kind]], place(kind, parts[n], s), own_sem.at[n, kind]
            )
            own[n, kind].start()

    pl.semaphore_wait(barrier, n_src - 1 + 3)

    tau_out = {}

    def send_tau(m, owner):
        tau_out[m] = go(remote(
            tau_part(owner), xbuf.at[:, :, c], tau_send.at[m], tau_recv.at[m], (s, flipped(c, m)),
        ))

    for copy in far[:HALF]:
        copy.start()
    send_tau(2, 1 - x)
    for kind in (0, 1):
        for i in range(HALF):
            lay_out(sendbuf, base + i, kind)
    send_direct(0, lambda i: sendbuf.at[i])
    send_tau(1, x)
    keep_own(0, sendbuf.at[s])
    for i in range(HALF):
        lay_out(sendbuf, away + i, 1)
    pick_rows(1, one_hot([base + i for i in range(HALF)]), HALF)
    for kind in (0, 1):
        for i in range(HALF):
            lay_out(sendother, i, kind)
    send_direct(1, lambda i: sendother.at[i - base])
    keep_own(1, sendother.at[s - base])

    def far_source(q):
        return (inner_at, outer_at)[q // 2] * 2 + flipped(lane_y, q % 2)

    near_in = []

    def to_near(ref, at):
        near_in.append(go(remote(ref, ref, near_send.at[at], near_recv.at[at], (s, near))))

    def pass_half(n):
        own[n, 0].wait()
        for m in (1, 2, 3):
            direct[n, 0, m].wait_recv()
        to_near(source_rows.at[parts[n], h, pl.ds(base, HALF)], n)

    relayed = {}

    def relay(kind, q):
        chunk = place(kind, x, far_source(q))
        remote(chunk, chunk, on_send.at[kind, q], far_recv.at[kind, q], (s, across)).wait_recv()
        relayed[kind, q] = go(remote(
            chunk, chunk, on_send.at[kind, q], on_recv.at[kind, q], (s, across)
        ))
        if kind == 0:
            to_near(chunk, 2 + q)

    def pass_on(q):
        relayed[0, q].wait_recv()
        to_near(place(0, 1 - x, far_source(q)), 6 + q)

    def pass_tau():
        tau_out[2].wait_recv()
        theirs = xbuf.at[:, :, across]
        tau_out[3] = go(remote(theirs, theirs, tau_pass_send, tau_pass_recv, (s, near)))

    def turn_tau():
        tau_in.wait()
        tau_out[1].wait_recv()
        tau_out[3].wait_recv()
        blocks = nv // rows

        def one(t, carry):
            for part in (0, 1):
                spun[part] = jnp.transpose(xbuf[part, t].reshape(nv, nv)).reshape(blocks, rows, nv)
            for i in range(n_src):
                down = slice(i * rows, (i + 1) * rows)
                re, im = spun[0, 2 * i + h], spun[1, 2 * i + h]
                turned[0, t, 0, down] = re
                turned[0, t, 1, down] = -im
                turned[1, t, 0, down] = im
                turned[1, t, 1, down] = re
            return carry

        lax.fori_loop(0, times, one, 0)

    def mm(a, b, dims):
        return lax.dot_general(a, b, dims, preferred_element_type=f32)

    def stacked(part, k):
        return jnp.concatenate(
            [source_rows[part, side, i, k] for i in range(n_src) for side in range(2)], axis=0
        )

    mid = nv // 2

    def rights(k, carry):
        e_re, e_im = stacked(0, k), stacked(1, k)
        for t in range(times):
            got = (
                mm(turned[0, t].reshape(nv, nv), e_re, NT) + mm(turned[1, t].reshape(nv, nv), e_im, NT)
            ).astype(bf16)
            right_pos[t, k, 0] = got[:mid]
            right_pos[t, k, 1] = got[mid:]
            right_neg[t, k, 0] = -got[mid:]
            right_neg[t, k, 1] = got[:mid]
        return carry

    def wholes(t, carry):
        x_re, x_im = xbuf[0, t].reshape(nv, nv), xbuf[1, t].reshape(nv, nv)
        for k in range(n_source):
            got = mm(right_pos[t, k].reshape(nv, nv), x_re, NN) + mm(
                right_neg[t, k].reshape(nv, nv), x_im, NN
            )
            xmat[t, k, 0] = got[:mid]
            xmat[t, k, 1] = got[mid:]
        return carry

    n_diag = diag_ref.shape[2]
    zero = jnp.zeros((8, 128), f32)

    def products(sources, first):
        for n, i in enumerate(sources):
            for part in (0, 1):
                for k in range(n_sink):
                    staged[n, part, k] = sink_rows[part, i, k].astype(f32)

        def one(d, carry):
            k1, k2 = diag_ref[0, 0, d], diag_ref[1, 0, d]
            acc = [zero if first else sums[d, n] for n in range(2 * times)]
            for n, i in enumerate(sources):
                e_re, e_im = staged[n, 0, k1], staged[n, 1, k1]
                down = pl.ds(pl.multiple_of(i * rows, rows), rows)
                for t in range(times):
                    x_re, x_im = xmat[t, k2, 0, down, :], xmat[t, k2, 1, down, :]
                    re = e_re * x_re - e_im * x_im
                    im = e_re * x_im + e_im * x_re
                    for m, value in ((2 * t, re), (2 * t + 1, im)):
                        for r in range(rows // 8):
                            for l in range(nv // 128):
                                acc[m] = acc[m] + value[r * 8:(r + 1) * 8, l * 128:(l + 1) * 128]
            for n in range(2 * times):
                sums[d, n] = acc[n]
            return carry

        lax.fori_loop(0, n_diag, one, 0)

    for n, q in enumerate((2, 3, 0, 1)):
        far[n].wait_send()
        far[HALF + n].start()
        relay(0, q)
    pass_on(2)
    pass_on(3)
    pass_half(0)
    pass_tau()
    pass_on(0)
    pass_half(1)
    pass_on(1)
    turn_tau()
    relay(1, 0)
    for copy in near_in:
        copy.wait_recv()
    lax.fori_loop(0, n_source // 2, rights, 0)
    relay(1, 1)
    relay(1, 2)
    lax.fori_loop(n_source // 2, n_source, rights, 0)
    wholes(0, 0)
    relay(1, 3)
    lax.fori_loop(1, times, wholes, 0)

    for copy in smalls[1:]:
        copy.wait()
    for n in (0, 1):
        own[n, 1].wait()
        for m in (1, 2, 3):
            direct[n, 1, m].wait_recv()
    width = 2 * n_diag
    sub8 = lax.broadcasted_iota(jnp.int32, (8, width), 0)
    lane8 = lax.broadcasted_iota(jnp.int32, (8, width), 1)
    cosine, sine = jnp.zeros((8, width), f32), jnp.zeros((8, width), f32)
    for d in range(n_diag):
        turn = phase_ref[diag_ref[2, 0, d]]
        cos_d = (turn == 0).astype(f32) - (turn == 2).astype(f32)
        sin_d = (turn == 1).astype(f32) - (turn == 3).astype(f32)
        cosine = jnp.where(lane8 % n_diag == d, cos_d, cosine)
        sine = jnp.where(lane8 == d, -sin_d, jnp.where(lane8 == n_diag + d, sin_d, sine))
    first, size = 0, 0
    for j in range(size_ref.shape[0]):
        first = first + jnp.where(j < c, size_ref[j], 0)
        size = size + jnp.where(j == c, size_ref[j], 0)
    products([base + i for i in range(HALF)], True)
    for q in (0, 1, 2, 3):
        relayed[1, q].wait_recv()
        products([far_source(q)], False)

    flat = jnp.concatenate(
        [
            jnp.sum(sums[d, 2 * t + n], axis=0, keepdims=True)
            for t in range(times) for n in (0, 1) for d in range(n_diag)
        ],
        axis=0,
    )
    flat = jnp.sum(jnp.transpose(flat), axis=0, keepdims=True)
    tile = jnp.zeros((8, width), f32)
    for t in range(times):
        tile = jnp.where(sub8 == x * times + t, flat[:, t * width:(t + 1) * width], tile)
    vbuf[c, :, :width] = tile

    val_out = []
    for m in (2, 3, 1):
        val_out.append(go(remote(
            vbuf.at[c], vbuf.at[c], val_send.at[m], val_recv.at[m], (s, flipped(c, m)),
        )))
    for copy in val_out:
        copy.wait_recv()

    whole = vbuf[0, :, :width]
    for n in range(1, vbuf.shape[0]):
        whole = whole + vbuf[n, :, :width]
    swapped = jnp.concatenate([whole[:, n_diag:], whole[:, :n_diag]], axis=1)
    total[:, :width] = cosine * whole + sine * swapped
    for at_place in range(MAXB):
        at = jnp.minimum(first + at_place, total.shape[0] - 1)
        keep = (at_place < size).astype(f32)
        row = total[pl.ds(at, 1), :width] * keep
        out_ref[at_place, 0:1, :] = row[:, :n_diag]
        out_ref[at_place, 1:2, :] = row[:, n_diag:]

    for copy in far[HALF:] + started:
        copy.wait_send()


def fused_local(tau_cols, elementals, need_ids, diagrams, phases, block_sizes):
    n_snk = lax.axis_size("snk")
    n_src, n_ids = need_ids.shape
    own_rows, _, ne, nv = elementals.shape
    sinks, cols = tau_cols.shape[2], tau_cols.shape[3]
    times = sinks // 2
    rows = own_rows // 2
    n_diag = diagrams.shape[1]
    n_right = n_ids - NSN
    bf16, f32 = jnp.bfloat16, jnp.float32
    sem = pltpu.SemaphoreType.DMA
    i32 = jnp.int32
    held = pl.BlockSpec(memory_space=pltpu.HBM)
    values = pl.pallas_call(
        kernel,
        out_shape=pltpu.VMEM((MAXB, 2, n_diag), f32),
        in_specs=[held] * 6,
        out_specs=pl.BlockSpec(memory_space=pltpu.VMEM),
        scratch_shapes=[
            pltpu.SMEM((n_src, n_ids), i32),
            pltpu.SMEM((3, 1, n_diag), i32),
            pltpu.SMEM(phases.shape, i32),
            pltpu.SMEM(block_sizes.shape, i32),
            pltpu.VMEM((2, rows, ne, nv), bf16),
            pltpu.VMEM((nv // 128, n_src * n_ids * rows, 128), f32),
            pltpu.VMEM((n_src, n_ids, rows, nv), bf16),
            pltpu.VMEM((HALF, n_ids, rows, nv), bf16),
            pltpu.VMEM((2, n_src, NSN, rows, nv), bf16),
            pltpu.VMEM((2, 2, n_src, n_right, rows, nv), bf16),
            pltpu.VMEM((2, times, n_snk, cols, nv), bf16),
            pltpu.VMEM((2, nv // rows, rows, nv), bf16),
            pltpu.VMEM((2, times, 2, nv // 2, nv), bf16),
            pltpu.VMEM((times, n_right, 2, nv // 2, nv), bf16),
            pltpu.VMEM((times, n_right, 2, nv // 2, nv), bf16),
            pltpu.VMEM((times, n_right, 2, nv // 2, nv), f32),
            pltpu.VMEM((HALF, 2, NSN, rows, nv), f32),
            pltpu.VMEM((n_diag, 2 * times, 8, 128), f32),
            pltpu.VMEM((n_snk, 8, 128), f32),
            pltpu.VMEM((8, 128), f32),
            sem((4,)), sem((2, PIECES)), sem((2, 2)), sem, sem((4,)), sem((4,)), sem, sem,
            sem((2, 2, 4)), sem((2, 2, 4)), sem((2, 4)), sem((2, 4)), sem((2, 4)), sem((2, 4)),
            sem((10,)), sem((10,)), sem((4,)), sem((4,)),
        ],
        compiler_params=pltpu.CompilerParams(
            collective_id=0, has_side_effects=True, vmem_limit_bytes=60 * 2**20
        ),
    )(need_ids, jnp.transpose(diagrams, (2, 0, 1)), phases, block_sizes, tau_cols, elementals)
    return values.reshape(1, 1, MAXB, 2, n_diag)


def local(tau_cols, elementals, *rest):
    fits = (
        lax.axis_size("snk") == 4
        and lax.axis_size("src") == 8
        and elementals.shape[0] == 32
        and tau_cols.shape[2] == 8
        and tau_cols.shape[3] == 64
        and tau_cols.shape[4] == 256
    )
    return (fused_local if fits else plain_local)(tau_cols, elementals, *rest)


def solution(mesh):
    placed = (
        P(None, "src", None, "snk", None),
        P("src", None, None, None),
        P(),
        P("src", None, None),
        P(),
        P(),
    )
    return jax.shard_map(
        local,
        mesh=mesh,
        in_specs=placed,
        out_specs=P("src", "snk", None, None, None),
        check_vma=False,
    )
```

```python
import functools

import jax
import jax.numpy as jnp
from jax import lax
from jax.experimental import pallas as pl
from jax.experimental.pallas import tpu as pltpu
from jax.sharding import PartitionSpec as P

NSN = 4
MAXB = 3


def slot_values(gathered, tau_slot, diagram_rows, phases):
    real_part = tau_slot[0]
    imag_part = tau_slot[1]
    left_stack = jnp.stack([jnp.stack([real_part, imag_part]), jnp.stack([-imag_part, real_part])])
    right_stack = jnp.stack([jnp.stack([real_part, -imag_part]), jnp.stack([imag_part, real_part])])
    left_node = lax.dot_general(
        gathered[:, :, :NSN],
        left_stack,
        (((1, 3), (0, 3)), ((), ())),
        preferred_element_type=jnp.float32,
    ).astype(jnp.bfloat16)
    right_node = lax.dot_general(
        gathered[:, :, NSN:],
        right_stack,
        (((1, 3), (0, 2)), ((), ())),
        preferred_element_type=jnp.float32,
    ).astype(jnp.bfloat16)
    pair_sums = lax.dot_general(
        left_node, right_node, (((0, 3), (3, 0)), ((), ())), preferred_element_type=jnp.float32
    )
    pair_real = pair_sums[:, 0, :, 0] - pair_sums[:, 1, :, 1]
    pair_imag = pair_sums[:, 0, :, 1] + pair_sums[:, 1, :, 0]
    sink_pick = (
        diagram_rows[:, 0:1] == jnp.arange(pair_real.shape[0], dtype=jnp.int32)[None, :]
    ).astype(jnp.float32)
    source_pick = (
        diagram_rows[:, 1:2] == jnp.arange(pair_real.shape[1], dtype=jnp.int32)[None, :]
    ).astype(jnp.float32)
    chosen_real = jnp.sum(
        sink_pick[:, :, None] * pair_real[None] * source_pick[:, None, :], axis=(1, 2)
    )
    chosen_imag = jnp.sum(
        sink_pick[:, :, None] * pair_imag[None] * source_pick[:, None, :], axis=(1, 2)
    )
    gamma_pick = diagram_rows[:, 2:3] == jnp.arange(phases.shape[0], dtype=jnp.int32)[None, :]
    quarter = jnp.sum(jnp.where(gamma_pick, phases[None, :], 0), axis=1)
    cosine = (quarter == 0).astype(jnp.float32) - (quarter == 2).astype(jnp.float32)
    sine_part = (quarter == 1).astype(jnp.float32) - (quarter == 3).astype(jnp.float32)
    return jnp.stack(
        [
            cosine * chosen_real - sine_part * chosen_imag,
            sine_part * chosen_real + cosine * chosen_imag,
        ]
    )


def plain_local(tau_cols, elementals, need_ids, diagrams, phases, block_sizes):
    groups = lax.axis_size("snk")
    column = lax.axis_index("snk")
    full_width = tau_cols.shape[4]
    col_count = tau_cols.shape[3]
    sink_count = tau_cols.shape[2]
    diagram_rows = diagrams[0]
    block_at = jnp.arange(block_sizes.shape[0], dtype=jnp.int32)
    starts = jnp.sum(
        jnp.where(block_at[None, :] < block_at[:, None], block_sizes[None, :], 0), axis=1
    )
    offsets = jnp.arange(MAXB, dtype=jnp.int32)
    picked = jnp.take(elementals, need_ids, axis=2)
    arrived = lax.all_to_all(picked, "src", split_axis=2, concat_axis=0, tiled=True)
    gathered = arrived.reshape(full_width, 2, need_ids.shape[1], full_width)
    local_tau = tau_cols[:, 0]
    per_group = sink_count // groups
    half_turn = groups // 2
    packed = local_tau.reshape(2, groups, per_group, col_count, full_width)
    packed = jnp.roll(packed, -half_turn, axis=1)
    arrived_tau = lax.all_to_all(packed, "snk", split_axis=1, concat_axis=3, tiled=True)
    blocks = arrived_tau.reshape(2, per_group, full_width, full_width)
    results = jnp.stack(
        [
            slot_values(gathered, blocks[:, place], diagram_rows, phases)
            for place in range(per_group)
        ]
    )
    all_values = lax.all_gather(results, "snk", axis=0, tiled=True)
    all_values = jnp.roll(all_values, half_turn * per_group, axis=0)
    own_start = lax.dynamic_index_in_dim(starts, column, keepdims=False)
    own_size = lax.dynamic_index_in_dim(block_sizes, column, keepdims=False)
    own_filled = offsets < own_size
    own_times = jnp.where(own_filled, own_start + offsets, 0)
    wanted = own_filled[:, None] & (
        own_times[:, None] == jnp.arange(all_values.shape[0], dtype=jnp.int32)[None, :]
    )
    correlators = jnp.sum(jnp.where(wanted[:, :, None, None], all_values[None], 0.0), axis=1)
    return correlators.reshape(1, 1, MAXB, 2, diagram_rows.shape[0])


MESH = pl.DeviceIdType.MESH
HALF = 4
PIECES = 2
NT = (((1,), (1,)), ((), ()))
NN = (((1,), (0,)), ((), ()))


def flipped(value, mask):
    for bit in (1, 2, 4):
        if mask & bit:
            value = value + bit * (1 - 2 * ((value // bit) % 2))
    return value


def kernel(
    ids_hbm, diag_hbm, phase_hbm, size_hbm, tau_ref, el_ref, out_ref,
    ids_ref, diag_ref, phase_ref, size_ref,
    table, pick, sendbuf, sendother, sink_rows, source_rows, xbuf,
    spun, turned, right_pos, right_neg, xmat, staged, sums, vbuf, total,
    small_sem, tab_sem, own_sem, tau_own, tau_send, tau_recv, tau_pass_send, tau_pass_recv,
    direct_send, direct_recv, far_send, far_recv, on_send, on_recv, near_send, near_recv,
    val_send, val_recv, late_sem,
):
    s = lax.axis_index("src")
    c = lax.axis_index("snk")
    x, h = c // 2, c % 2
    n_src, n_ids = ids_ref.shape
    rows, ne, nv = table.shape[1:]
    times = xbuf.shape[1]
    f32, bf16 = jnp.float32, jnp.bfloat16
    base = (s // HALF) * HALF
    near, across = flipped(c, 1), flipped(c, 2)
    n_sink, n_source = sink_rows.shape[2], source_rows.shape[3]
    ids_of = (pl.ds(n_sink, n_source), pl.ds(0, n_sink))

    smalls = []
    for n, (there, here) in enumerate(
        ((ids_hbm, ids_ref), (diag_hbm, diag_ref), (phase_hbm, phase_ref), (size_hbm, size_ref))
    ):
        smalls.append(pltpu.make_async_copy(there, here, small_sem.at[n]))
        smalls[-1].start()
    parts = (x, 1 - x)
    table_in = []
    for n, part in enumerate(parts):
        table_in.append([])
        for piece in range(PIECES):
            step = rows // PIECES
            table_in[n].append(
                pltpu.make_async_copy(
                    el_ref.at[pl.ds(h * rows + piece * step, step), part],
                    table.at[n, pl.ds(piece * step, step)], tab_sem.at[n, piece],
                )
            )
            table_in[n][piece].start()

    barrier = pltpu.get_barrier_semaphore()
    depth = s // 2
    last = n_src // 2 - 1

    def greet(semaphore, m):
        pl.semaphore_signal(semaphore, 1, device_id=(flipped(s, m), c), device_id_type=MESH)

    for m in range(1, n_src):
        if m in (2, 3):
            pl.when(depth != last)(functools.partial(greet, barrier, m))
        else:
            greet(barrier, m)
    for m in range(1, 4):
        pl.semaphore_signal(barrier, 1, device_id=(s, flipped(c, m)), device_id_type=MESH)

    def tau_part(owner):
        return tau_ref.at[:, 0, pl.ds(owner * times, times)]

    tau_in = pltpu.make_async_copy(tau_part(x), xbuf.at[:, :, c], tau_own)
    tau_in.start()

    sub = lax.broadcasted_iota(jnp.int32, (n_ids, ne), 0)
    lane = lax.broadcasted_iota(jnp.int32, (n_ids, ne), 1)
    smalls[0].wait()

    def one_hot(owners):
        hots = []
        for i in owners:
            wanted = jnp.zeros((n_ids, ne), jnp.int32)
            for k in range(n_ids):
                wanted = jnp.where(sub == k, ids_ref[i, k], wanted)
            hots.append((wanted == lane).astype(f32))
        return jnp.concatenate(hots, axis=0).astype(bf16)

    def pick_rows(n, hot, count):
        for r in range(rows):
            if r % (rows // PIECES) == 0:
                table_in[n][r // (rows // PIECES)].wait()
            got = lax.dot_general(hot, table[n, r], NN, preferred_element_type=f32)
            for side in range(nv // 128):
                pick[side, pl.ds(r, count * n_ids, stride=rows), :] = got[:, side * 128:(side + 1) * 128]

    def lay_out(target, i, kind):
        first, count = (n_sink, n_source) if kind == 0 else (0, n_sink)
        down = pl.ds(pl.multiple_of((i * n_ids + first) * rows, rows), count * rows)
        for side in range(nv // 128):
            target[i, ids_of[kind], :, side * 128:(side + 1) * 128] = (
                pick[side, down, :].astype(bf16).reshape(count, rows, 128)
            )

    def remote(src, dst, send, recv, device):
        return pltpu.make_async_remote_copy(
            src_ref=src, dst_ref=dst, send_sem=send, recv_sem=recv,
            device_id=device, device_id_type=MESH,
        )

    started = []

    def go(copy):
        copy.start()
        started.append(copy)
        return copy

    def place(kind, part, source):
        return source_rows.at[part, h, source] if kind == 0 else sink_rows.at[part, source]

    away = HALF - base
    pick_rows(0, one_hot(range(n_src)), n_src)
    for i in range(HALF):
        lay_out(sendbuf, away + i, 0)

    lane_y = s % 2
    inner = ((depth + 1) // 2) % 2
    other_half = 1 - depth // 2
    inner_at, outer_at = 1 + other_half, 3 * other_half

    far = []
    for kind in (0, 1):
        for n, there, y in ((1, outer_at, 0), (0, inner_at, 0), (1, outer_at, 1), (0, inner_at, 1)):
            y_flip = (y + lane_y) % 2
            far.append(remote(
                sendbuf.at[there * 2 + y, ids_of[kind]], place(kind, x, s),
                far_send.at[kind, 2 * n + y], far_recv.at[kind, 2 * (1 - inner) + y_flip],
                (there * 2 + y, c),
            ))

    direct = {}

    def send_direct(n, chunk_of):
        for kind in (0, 1):
            for m in (2, 3, 1):
                direct[n, kind, m] = remote(
                    chunk_of(flipped(s, m)).at[ids_of[kind]], place(kind, parts[n], s),
                    direct_send.at[n, kind, m], direct_recv.at[n, kind, m], (flipped(s, m), c),
                )
                go(direct[n, kind, m])

    own = {}

    def keep_own(n, chunk):
        for kind in (0, 1):
            own[n, kind] = pltpu.make_async_copy(
                chunk.at[ids_of[kind]], place(kind, parts[n], s), own_sem.at[n, kind]
            )
            own[n, kind].start()

    @pl.when(depth != last - 1)
    def _():
        pl.semaphore_wait(barrier, n_src - 1 + 3)

    @pl.when(depth == last - 1)
    def _():
        pl.semaphore_wait(barrier, n_src - 1 + 1)

    @pl.when(depth == last)
    def _():
        for m in (2, 3):
            greet(late_sem, m)


    tau_out = {}

    def send_tau(m, owner):
        tau_out[m] = go(remote(
            tau_part(owner), xbuf.at[:, :, c], tau_send.at[m], tau_recv.at[m], (s, flipped(c, m)),
        ))

    for copy in far[:HALF]:
        copy.start()
    send_tau(2, 1 - x)
    for kind in (0, 1):
        for i in range(HALF):
            lay_out(sendbuf, base + i, kind)

    @pl.when(depth == last - 1)
    def _():
        pl.semaphore_wait(late_sem, 2)

    send_direct(0, lambda i: sendbuf.at[i])
    send_tau(1, x)
    keep_own(0, sendbuf.at[s])
    for i in range(HALF):
        lay_out(sendbuf, away + i, 1)
    pick_rows(1, one_hot([base + i for i in range(HALF)]), HALF)
    for kind in (0, 1):
        for i in range(HALF):
            lay_out(sendother, i, kind)
    send_direct(1, lambda i: sendother.at[i - base])
    keep_own(1, sendother.at[s - base])

    def far_source(q):
        return (inner_at, outer_at)[q // 2] * 2 + flipped(lane_y, q % 2)

    near_in = []

    def to_near(ref, at):
        near_in.append(go(remote(ref, ref, near_send.at[at], near_recv.at[at], (s, near))))

    def pass_half(n):
        own[n, 0].wait()
        for m in (1, 2, 3):
            direct[n, 0, m].wait_recv()
        to_near(source_rows.at[parts[n], h, pl.ds(base, HALF)], n)

    relayed = {}

    def relay(kind, q):
        chunk = place(kind, x, far_source(q))
        remote(chunk, chunk, on_send.at[kind, q], far_recv.at[kind, q], (s, across)).wait_recv()
        relayed[kind, q] = go(remote(
            chunk, chunk, on_send.at[kind, q], on_recv.at[kind, q], (s, across)
        ))
        if kind == 0:
            to_near(chunk, 2 + q)

    def pass_on(q):
        relayed[0, q].wait_recv()
        to_near(place(0, 1 - x, far_source(q)), 6 + q)

    def pass_tau():
        tau_out[2].wait_recv()
        theirs = xbuf.at[:, :, across]
        tau_out[3] = go(remote(theirs, theirs, tau_pass_send, tau_pass_recv, (s, near)))

    def turn_tau():
        tau_in.wait()
        tau_out[1].wait_recv()
        tau_out[3].wait_recv()
        blocks = nv // rows

        def one(t, carry):
            for part in (0, 1):
                spun[part] = jnp.transpose(xbuf[part, t].reshape(nv, nv)).reshape(blocks, rows, nv)
            for i in range(n_src):
                down = slice(i * rows, (i + 1) * rows)
                re, im = spun[0, 2 * i + h], spun[1, 2 * i + h]
                turned[0, t, 0, down] = re
                turned[0, t, 1, down] = -im
                turned[1, t, 0, down] = im
                turned[1, t, 1, down] = re
            return carry

        lax.fori_loop(0, times, one, 0)

    def mm(a, b, dims):
        return lax.dot_general(a, b, dims, preferred_element_type=f32)

    def stacked(part, k):
        return jnp.concatenate(
            [source_rows[part, side, i, k] for i in range(n_src) for side in range(2)], axis=0
        )

    mid = nv // 2

    def rights(k, carry):
        e_re, e_im = stacked(0, k), stacked(1, k)
        for t in range(times):
            got = (
                mm(turned[0, t].reshape(nv, nv), e_re, NT) + mm(turned[1, t].reshape(nv, nv), e_im, NT)
            ).astype(bf16)
            right_pos[t, k, 0] = got[:mid]
            right_pos[t, k, 1] = got[mid:]
            right_neg[t, k, 0] = -got[mid:]
            right_neg[t, k, 1] = got[:mid]
        return carry

    def wholes(t, carry):
        x_re, x_im = xbuf[0, t].reshape(nv, nv), xbuf[1, t].reshape(nv, nv)
        for k in range(n_source):
            got = mm(right_pos[t, k].reshape(nv, nv), x_re, NN) + mm(
                right_neg[t, k].reshape(nv, nv), x_im, NN
            )
            xmat[t, k, 0] = got[:mid]
            xmat[t, k, 1] = got[mid:]
        return carry

    n_diag = diag_ref.shape[2]
    zero = jnp.zeros((8, 128), f32)

    def products(sources, first):
        for n, i in enumerate(sources):
            for part in (0, 1):
                for k in range(n_sink):
                    staged[n, part, k] = sink_rows[part, i, k].astype(f32)

        def one(d, carry):
            k1, k2 = diag_ref[0, 0, d], diag_ref[1, 0, d]
            acc = [zero if first else sums[d, n] for n in range(2 * times)]
            for n, i in enumerate(sources):
                e_re, e_im = staged[n, 0, k1], staged[n, 1, k1]
                down = pl.ds(pl.multiple_of(i * rows, rows), rows)
                for t in range(times):
                    x_re, x_im = xmat[t, k2, 0, down, :], xmat[t, k2, 1, down, :]
                    re = e_re * x_re - e_im * x_im
                    im = e_re * x_im + e_im * x_re
                    for m, value in ((2 * t, re), (2 * t + 1, im)):
                        for r in range(rows // 8):
                            for l in range(nv // 128):
                                acc[m] = acc[m] + value[r * 8:(r + 1) * 8, l * 128:(l + 1) * 128]
            for n in range(2 * times):
                sums[d, n] = acc[n]
            return carry

        lax.fori_loop(0, n_diag, one, 0)

    for n, q in enumerate((2, 3, 0, 1)):
        far[n].wait_send()
        far[HALF + n].start()
        relay(0, q)
    pass_on(2)
    pass_on(3)
    pass_half(0)
    pass_tau()
    pass_on(0)
    pass_half(1)
    pass_on(1)
    turn_tau()
    relay(1, 0)
    for copy in near_in:
        copy.wait_recv()
    lax.fori_loop(0, n_source // 2, rights, 0)
    relay(1, 1)
    relay(1, 2)
    lax.fori_loop(n_source // 2, n_source, rights, 0)
    wholes(0, 0)
    relay(1, 3)
    lax.fori_loop(1, times, wholes, 0)

    for copy in smalls[1:]:
        copy.wait()
    for n in (0, 1):
        own[n, 1].wait()
        for m in (1, 2, 3):
            direct[n, 1, m].wait_recv()
    width = 2 * n_diag
    sub8 = lax.broadcasted_iota(jnp.int32, (8, width), 0)
    lane8 = lax.broadcasted_iota(jnp.int32, (8, width), 1)
    cosine, sine = jnp.zeros((8, width), f32), jnp.zeros((8, width), f32)
    for d in range(n_diag):
        turn = phase_ref[diag_ref[2, 0, d]]
        cos_d = (turn == 0).astype(f32) - (turn == 2).astype(f32)
        sin_d = (turn == 1).astype(f32) - (turn == 3).astype(f32)
        cosine = jnp.where(lane8 % n_diag == d, cos_d, cosine)
        sine = jnp.where(lane8 == d, -sin_d, jnp.where(lane8 == n_diag + d, sin_d, sine))
    first, size = 0, 0
    for j in range(size_ref.shape[0]):
        first = first + jnp.where(j < c, size_ref[j], 0)
        size = size + jnp.where(j == c, size_ref[j], 0)
    products([base + i for i in range(HALF)], True)
    for q in (0, 1, 2, 3):
        relayed[1, q].wait_recv()
        products([far_source(q)], False)

    flat = jnp.concatenate(
        [
            jnp.sum(sums[d, 2 * t + n], axis=0, keepdims=True)
            for t in range(times) for n in (0, 1) for d in range(n_diag)
        ],
        axis=0,
    )
    flat = jnp.sum(jnp.transpose(flat), axis=0, keepdims=True)
    tile = jnp.zeros((8, width), f32)
    for t in range(times):
        tile = jnp.where(sub8 == x * times + t, flat[:, t * width:(t + 1) * width], tile)
    vbuf[c, :, :width] = tile

    val_out = []
    for m in (2, 3, 1):
        val_out.append(go(remote(
            vbuf.at[c], vbuf.at[c], val_send.at[m], val_recv.at[m], (s, flipped(c, m)),
        )))
    for copy in val_out:
        copy.wait_recv()

    whole = vbuf[0, :, :width]
    for n in range(1, vbuf.shape[0]):
        whole = whole + vbuf[n, :, :width]
    swapped = jnp.concatenate([whole[:, n_diag:], whole[:, :n_diag]], axis=1)
    total[:, :width] = cosine * whole + sine * swapped
    for at_place in range(MAXB):
        at = jnp.minimum(first + at_place, total.shape[0] - 1)
        keep = (at_place < size).astype(f32)
        row = total[pl.ds(at, 1), :width] * keep
        out_ref[at_place, 0:1, :] = row[:, :n_diag]
        out_ref[at_place, 1:2, :] = row[:, n_diag:]

    for copy in far[HALF:] + started:
        copy.wait_send()


def fused_local(tau_cols, elementals, need_ids, diagrams, phases, block_sizes):
    n_snk = lax.axis_size("snk")
    n_src, n_ids = need_ids.shape
    own_rows, _, ne, nv = elementals.shape
    sinks, cols = tau_cols.shape[2], tau_cols.shape[3]
    times = sinks // 2
    rows = own_rows // 2
    n_diag = diagrams.shape[1]
    n_right = n_ids - NSN
    bf16, f32 = jnp.bfloat16, jnp.float32
    sem = pltpu.SemaphoreType.DMA
    i32 = jnp.int32
    held = pl.BlockSpec(memory_space=pltpu.HBM)
    values = pl.pallas_call(
        kernel,
        out_shape=pltpu.VMEM((MAXB, 2, n_diag), f32),
        in_specs=[held] * 6,
        out_specs=pl.BlockSpec(memory_space=pltpu.VMEM),
        scratch_shapes=[
            pltpu.SMEM((n_src, n_ids), i32),
            pltpu.SMEM((3, 1, n_diag), i32),
            pltpu.SMEM(phases.shape, i32),
            pltpu.SMEM(block_sizes.shape, i32),
            pltpu.VMEM((2, rows, ne, nv), bf16),
            pltpu.VMEM((nv // 128, n_src * n_ids * rows, 128), f32),
            pltpu.VMEM((n_src, n_ids, rows, nv), bf16),
            pltpu.VMEM((HALF, n_ids, rows, nv), bf16),
            pltpu.VMEM((2, n_src, NSN, rows, nv), bf16),
            pltpu.VMEM((2, 2, n_src, n_right, rows, nv), bf16),
            pltpu.VMEM((2, times, n_snk, cols, nv), bf16),
            pltpu.VMEM((2, nv // rows, rows, nv), bf16),
            pltpu.VMEM((2, times, 2, nv // 2, nv), bf16),
            pltpu.VMEM((times, n_right, 2, nv // 2, nv), bf16),
            pltpu.VMEM((times, n_right, 2, nv // 2, nv), bf16),
            pltpu.VMEM((times, n_right, 2, nv // 2, nv), f32),
            pltpu.VMEM((HALF, 2, NSN, rows, nv), f32),
            pltpu.VMEM((n_diag, 2 * times, 8, 128), f32),
            pltpu.VMEM((n_snk, 8, 128), f32),
            pltpu.VMEM((8, 128), f32),
            sem((4,)), sem((2, PIECES)), sem((2, 2)), sem, sem((4,)), sem((4,)), sem, sem,
            sem((2, 2, 4)), sem((2, 2, 4)), sem((2, 4)), sem((2, 4)), sem((2, 4)), sem((2, 4)),
            sem((10,)), sem((10,)), sem((4,)), sem((4,)), pltpu.SemaphoreType.REGULAR,
        ],
        compiler_params=pltpu.CompilerParams(
            collective_id=0, has_side_effects=True, vmem_limit_bytes=60 * 2**20
        ),
    )(need_ids, jnp.transpose(diagrams, (2, 0, 1)), phases, block_sizes, tau_cols, elementals)
    return values.reshape(1, 1, MAXB, 2, n_diag)


def local(tau_cols, elementals, *rest):
    fits = (
        lax.axis_size("snk") == 4
        and lax.axis_size("src") == 8
        and elementals.shape[0] == 32
        and tau_cols.shape[2] == 8
        and tau_cols.shape[3] == 64
        and tau_cols.shape[4] == 256
    )
    return (fused_local if fits else plain_local)(tau_cols, elementals, *rest)


def solution(mesh):
    placed = (
        P(None, "src", None, "snk", None),
        P("src", None, None, None),
        P(),
        P("src", None, None),
        P(),
        P(),
    )
    return jax.shard_map(
        local,
        mesh=mesh,
        in_specs=placed,
        out_specs=P("src", "snk", None, None, None),
        check_vma=False,
    )
```
